32 devices in a mesh: ctx: 8 (over y, x, core), tp: 4 (over z).
Axes of the slice: x: 2, y: 2, z: 4, core: 2. Of those that a mesh axis runs over, the one named last changes fastest.
Arguments:
- inputs: bfloat16 [4096, 2048], P(('ctx', 'tp')), may hold values from -54 to 54
- norm_gain: float32 [2048], replicated, may hold values from 0.1 to 1.9
- qkv_weight: bfloat16 [2048, 3, 2048], P(None, None, 'tp'), may hold values from -0.125 to 0.125
- head_gain: float32 [2048], P('tp'), may hold values from 0.1 to 1.9
- out_weight: bfloat16 [2048, 2048], P('tp'), may hold values from -0.125 to 0.125
- out_cotangent: bfloat16 [4096, 2048], P(('ctx', 'tp')), may hold values from -6 to 6
Outputs:
- outputs: bfloat16 [4096, 2048], P(('ctx', 'tp'))
- input_grad: bfloat16 [4096, 2048], P(('ctx', 'tp'))
- qkv_grad: float32 [2048, 3, 2048], P('ctx', None, 'tp')
- out_grad_t: float32 [2048, 2048], P('ctx', 'tp')
The draws below stay inside these ranges and needn't reach their ends.
All inputs are finite; a program needn't handle non-finite values.
Results may differ from the reference program's by a relative error of at most 0.015.
The reference program's roundings to bfloat16 on the way (of `normed`, `projected`, `scores`, `mixed`, `grad_attended`, `grad_scores` and `grad_proj`) count: a program that leaves them out, or rounds other values in their place, can miss the bound.
Values may be sent and summed in bfloat16 or wider, within the bound.
A program may use at most 128 MiB of HBM per device.

```python
import math
import jax
import jax.numpy as jnp
from jax import lax

D = 2048
H = 16
DH = 128
GROUP = 512
TOKENS = 4096


def draw_inputs(key, part):
    base_key, row_key, column_key = jax.random.split(key, 3)
    base = jax.random.truncated_normal(base_key, -6.0, 6.0, (TOKENS, D), jnp.float32)
    row_scales = jnp.exp(jax.random.uniform(row_key, (TOKENS, 1), jnp.float32, math.log(0.3), math.log(3.0)))
    column_scales = jnp.exp(jax.random.uniform(column_key, (1, D), jnp.float32, math.log(0.3), math.log(3.0)))
    return (base * row_scales * column_scales).astype(jnp.bfloat16)


def spiked(drawn, stream_key, source, target, blocks, factor):
    def block_of(dim):
        return (jnp.arange(drawn.shape[dim]) // (drawn.shape[dim] // blocks)).reshape((-1,) + (1,) * (drawn.ndim - 1 - dim))

    near = jax.random.permutation(stream_key, blocks)[block_of(target)]
    second = (block_of(target) + blocks // 2) % blocks
    return jnp.where((block_of(source) == near) | (block_of(source) == second), factor * drawn, drawn)


def level_of(rng, dims, shards, low, high):
    loudness = 1.0
    for position, blocks in shards:
        heights = jax.random.uniform(jax.random.fold_in(jax.random.fold_in(rng, 6), position), (blocks,), jnp.float32, low / len(shards), high / len(shards))
        loudness = loudness * jnp.repeat(jnp.exp(heights), dims[position] // blocks).reshape((-1,) + (1,) * (len(dims) - 1 - position))
    return loudness


def gaussian(stream_key, shape, deviation, limit, shards=(), dtype=jnp.bfloat16):
    result = jax.random.normal(stream_key, shape, jnp.float32) * deviation
    if len(shards) > 0:
        result = level_of(stream_key, shape, shards, -0.22, 0.18) * result
    return jnp.clip(result, min=-limit, max=limit).astype(dtype)


def bell_draw_with(stream_key, extent, scale, most, pieces, heavy, held_as=jnp.bfloat16):
    result = scale * jax.random.normal(stream_key, extent, jnp.float32)
    if pieces:
        result = result * level_of(stream_key, extent, pieces, -0.22, 0.18)
    return jnp.clip(spiked(result, jax.random.fold_in(stream_key, 3), *heavy), -most, most).astype(held_as)


def setup_inputs(seed: int = 0) -> dict:
    keys = jax.random.split(jax.random.key(seed), 7)
    inputs = draw_inputs(jax.random.fold_in(keys[6], 71), 0)
    norm_gain = jnp.clip(1.0 + 0.18 * jax.random.normal(keys[1], (D,), jnp.float32), 0.1, 1.9)
    qkv_weight = gaussian(keys[2], (D, 3, D), D ** -0.5, 0.125, ((2, 4),))
    head_gain = jnp.clip(1.0 + 0.18 * jax.random.normal(keys[3], (D,), jnp.float32), 0.1, 1.9)
    out_weight = gaussian(keys[4], (D, D), D ** -0.5, 0.125, ((0, 4),))
    out_cotangent = bell_draw_with(keys[5], (TOKENS, D), 1.0, 6.0, ((0, 32),), (0, 1, 32, 2.75))
    return {"inputs": inputs, "norm_gain": norm_gain, "qkv_weight": qkv_weight, "head_gain": head_gain, "out_weight": out_weight, "out_cotangent": out_cotangent}


EPSILON = 1e-05
highest = lax.Precision.HIGHEST

def row_scale(rows):
    return lax.rsqrt(lax.optimization_barrier(jnp.mean(rows * rows, axis=-1, keepdims=True)) + EPSILON)

def rounded(value):
    return lax.optimization_barrier(value.astype(jnp.bfloat16))

def masked_scores(query, key_block):
    causal = jnp.arange(GROUP)[:, None] >= jnp.arange(GROUP)[None, :]
    raw = jnp.einsum('thd,shd->hts', query, key_block, precision=highest)
    return rounded(jnp.where(causal[None], raw, 0.0)).astype(jnp.float32)

def reference(inputs, norm_gain, qkv_weight, head_gain, out_weight, out_cotangent):
    tokens_all = inputs.shape[0]
    width = inputs.shape[1]
    blocks = tokens_all // GROUP
    factor = 1.0 / math.sqrt(TOKENS)
    inputs_f = inputs.astype(jnp.float32)
    scale_in = row_scale(inputs_f)
    normed = rounded(inputs_f * scale_in * norm_gain)
    flat_weight = qkv_weight.reshape(width, 3 * width)
    projected = rounded(jnp.dot(normed, flat_weight, preferred_element_type=jnp.float32))
    split_parts = projected.reshape(blocks, GROUP, 3, H, DH).astype(jnp.float32)
    queries = split_parts[:, :, 0]
    key_rows = split_parts[:, :, 1]
    values = split_parts[:, :, 2]
    block_states = jnp.einsum('bshd,bshe->bhde', key_rows, values, precision=highest)
    zero_state = jnp.zeros_like(block_states[:1])
    states = jnp.concatenate([zero_state, jnp.cumsum(block_states, axis=0)[:-1]], axis=0)

    def forward_block(item):
        query, key_block, value, state = item
        scores = masked_scores(query, key_block)
        local_part = jnp.einsum('hts,she->the', scores, value, precision=highest)
        carried = jnp.einsum('thd,hde->the', query, state, precision=highest)
        return local_part + carried
    attended = lax.map(forward_block, (queries, key_rows, values, states))
    scale_head = row_scale(attended)
    gains = head_gain.reshape(H, DH)
    mixed = rounded(attended * scale_head * gains).reshape(tokens_all, width)
    outputs = (inputs_f + jnp.dot(mixed, out_weight, preferred_element_type=jnp.float32)).astype(jnp.bfloat16)
    grad_mixed = jnp.dot(out_cotangent, out_weight.T, preferred_element_type=jnp.float32).reshape(blocks, GROUP, H, DH)
    weighted = grad_mixed * gains
    cube_head = scale_head * scale_head * scale_head
    grad_attended = rounded(scale_head * weighted - cube_head * attended * lax.optimization_barrier(jnp.mean(weighted * attended, axis=-1, keepdims=True))).astype(jnp.float32)
    grad_blocks = jnp.einsum('bthd,bthe->bhde', queries, grad_attended, precision=highest)
    reversed_sums = jnp.cumsum(grad_blocks[::-1], axis=0)[::-1]
    grad_states = jnp.concatenate([reversed_sums[1:], zero_state], axis=0)

    def backward_block(item):
        query, key_block, value, grad_part, state, grad_state = item
        causal = jnp.arange(GROUP)[:, None] >= jnp.arange(GROUP)[None, :]
        scores = masked_scores(query, key_block)
        raw = jnp.einsum('the,she->hts', grad_part, value, precision=highest)
        grad_scores = rounded(jnp.where(causal[None], raw, 0.0)).astype(jnp.float32)
        grad_query = jnp.einsum('hts,shd->thd', grad_scores, key_block, precision=highest) + jnp.einsum('the,hde->thd', grad_part, state, precision=highest)
        grad_key = jnp.einsum('hts,thd->shd', grad_scores, query, precision=highest) + jnp.einsum('she,hde->shd', value, grad_state, precision=highest)
        grad_value = jnp.einsum('hts,the->she', scores, grad_part, precision=highest) + jnp.einsum('shd,hde->she', key_block, grad_state, precision=highest)
        return jnp.stack([grad_query, grad_key, grad_value], axis=1)
    grad_all = lax.map(backward_block, (queries, key_rows, values, grad_attended, states, grad_states))
    grad_proj = rounded(grad_all).reshape(tokens_all, 3 * width)
    grad_normed = jnp.dot(grad_proj, flat_weight.T, preferred_element_type=jnp.float32)
    weighted_in = grad_normed * norm_gain
    cube_in = scale_in * scale_in * scale_in
    input_grad = (out_cotangent.astype(jnp.float32) + scale_in * weighted_in - cube_in * inputs_f * lax.optimization_barrier(jnp.mean(weighted_in * inputs_f, axis=-1, keepdims=True))).astype(jnp.bfloat16)
    qkv_grad = jnp.dot(normed.T, grad_proj, preferred_element_type=jnp.float32).reshape(width, 3, width) * factor
    out_grad_t = jnp.dot(out_cotangent.T, mixed, preferred_element_type=jnp.float32) * factor
    return (outputs, input_grad, qkv_grad, out_grad_t)
```

```python
import functools
import math

import jax
import jax.numpy as jnp
from jax import lax
from jax.experimental import pallas as pl
from jax.experimental.pallas import tpu as pltpu
from jax.sharding import PartitionSpec as P

DH = 128
EPSILON = 1e-05
MESH = pl.DeviceIdType.MESH
F32 = jnp.float32
BF16 = jnp.bfloat16
VMEM_LIMIT = 63 * 1024 * 1024
NN = (((1,), (0,)), ((), ()))
NT = (((1,), (1,)), ((), ()))
TN = (((0,), (0,)), ((), ()))


def dot(a, b, dims=NN):
    return lax.dot_general(a, b, dims, preferred_element_type=F32)


def row_scale(rows):
    return lax.rsqrt(jnp.mean(rows * rows, axis=-1, keepdims=True) + EPSILON)


def split(value):
    high = value.astype(BF16)
    return high, (value - high.astype(F32)).astype(BF16)


def line_barrier(ctx, me, n, others):
    barrier = pltpu.get_barrier_semaphore()

    @pl.when(me > 0)
    def _():
        pl.semaphore_signal(barrier, inc=1, device_id=(ctx, me - 1), device_id_type=MESH)

    @pl.when(me < n - 1)
    def _():
        pl.semaphore_signal(barrier, inc=1, device_id=(ctx, me + 1), device_id_type=MESH)

    for other in others:
        pl.semaphore_signal(barrier, inc=1, device_id=(other, me), device_id_type=MESH)
    inner = jnp.logical_and(me > 0, me < n - 1)

    @pl.when(inner)
    def _():
        pl.semaphore_wait(barrier, 2 + len(others))

    @pl.when(jnp.logical_not(inner))
    def _():
        pl.semaphore_wait(barrier, 1 + len(others))


class LineGather:
    def __init__(self, ctx, me, n, own, held, send, recv):
        self.ctx, self.me, self.n = ctx, me, n
        self.own, self.held, self.send, self.recv = own, held, send, recv

    def at(self, origin):
        rows = self.own.shape[0]
        return self.held.at[pl.ds(pl.multiple_of(origin * rows, rows), rows), :]

    def copy(self, source, origin, up):
        target = self.me + 1 if up else self.me - 1
        return pltpu.make_async_remote_copy(
            src_ref=source,
            dst_ref=self.at(origin),
            send_sem=self.send.at[1 if up else 0, origin],
            recv_sem=self.recv.at[origin],
            device_id=(self.ctx, target),
            device_id_type=MESH,
        )

    def start_up(self):
        @pl.when(self.me < self.n - 1)
        def _():
            self.copy(self.own, self.me, True).start()

    def start_down(self):
        @pl.when(self.me > 0)
        def _():
            self.copy(self.own, self.me, False).start()

    def step(self, d):
        below, above = self.me - d, self.me + d

        @pl.when(below >= 0)
        def _():
            self.copy(self.at(below), below, True).wait_recv()

            @pl.when(self.me < self.n - 1)
            def _():
                self.copy(self.at(below), below, True).start()

        @pl.when(above < self.n)
        def _():
            self.copy(self.at(above), above, False).wait_recv()

            @pl.when(self.me > 0)
            def _():
                self.copy(self.at(above), above, False).start()

    def finish(self):
        for origin in range(self.n):

            @pl.when(jnp.logical_and(origin <= self.me, self.me < self.n - 1))
            def _():
                self.copy(self.at(origin), origin, True).wait_send()

            @pl.when(jnp.logical_and(origin >= self.me, self.me > 0))
            def _():
                self.copy(self.at(origin), origin, False).wait_send()


class LineScatter:
    def __init__(self, ctx, me, n, partial, total, out, arrived, send, recv):
        self.ctx, self.me, self.n = ctx, me, n
        self.partial, self.total, self.out = partial, total, out
        self.arrived = arrived
        self.send, self.recv = send, recv

    def copy(self, t, up, slot):
        target = self.me + 1 if up else self.me - 1
        return pltpu.make_async_remote_copy(
            src_ref=self.out.at[t],
            dst_ref=self.arrived.at[slot],
            send_sem=self.send.at[t],
            recv_sem=self.recv.at[slot],
            device_id=(self.ctx, target),
            device_id_type=MESH,
        )

    def add(self, slot):
        self.copy(0, True, slot).wait_recv()
        self.total[...] += self.arrived[slot].astype(F32)

    def step(self, s):
        me, n = self.me, self.n

        @pl.when(s >= me)
        def _():
            t = n - 1 - s + me
            self.partial(t, self.total)

            @pl.when(me > 0)
            def _():
                self.add(t)

            self.out[t] = self.total[...].astype(BF16)
            self.copy(t, True, t).start()

        @pl.when(s >= n - 1 - me)
        def _():
            t = s - (n - 1 - me)
            self.partial(t, self.total)

            @pl.when(me < n - 1)
            def _():
                self.add(t)

            self.out[t] = self.total[...].astype(BF16)
            self.copy(t, False, n if s == n - 2 else t).start()

    def finish(self):
        me, n = self.me, self.n
        self.partial(me, self.total)

        @pl.when(me > 0)
        def _():
            self.add(me)

        @pl.when(me < n - 1)
        def _():
            self.add(n)

        for t in range(n):

            @pl.when(t != me)
            def _():
                self.copy(t, True, t).wait_send()


class StateSum:
    def __init__(self, ctx, me, chips, later, local, mine, pair, chip_sum, arrived, sems):
        self.chip, self.core = ctx // 2, lax.rem(ctx, 2)
        self.sibling = ctx + 1 - 2 * self.core
        self.me, self.chips, self.later = me, chips, later
        self.local, self.mine, self.pair = local, mine, pair
        self.chip_sum, self.arrived, self.sems = chip_sum, arrived, sems

    def pair_copy(self):
        return pltpu.make_async_remote_copy(
            src_ref=self.mine,
            dst_ref=self.pair,
            send_sem=self.sems.at[0, 0],
            recv_sem=self.sems.at[1, 0],
            device_id=(self.sibling, self.me),
            device_id_type=MESH,
        )

    def chip_copy(self, target, origin):
        return pltpu.make_async_remote_copy(
            src_ref=self.chip_sum,
            dst_ref=self.arrived.at[origin],
            send_sem=self.sems.at[0, target + 1],
            recv_sem=self.sems.at[1, origin + 1],
            device_id=(2 * target + self.core, self.me),
            device_id_type=MESH,
        )

    def wanted(self, source, target):
        return source > target if self.later else source < target

    def start(self):
        self.mine[...] = self.local[...].astype(BF16)
        self.pair_copy().start()

    def spread(self):
        self.pair_copy().wait()
        self.chip_sum[...] = (self.local[...] + self.pair[...].astype(F32)).astype(BF16)
        for other in range(self.chips):

            @pl.when(self.wanted(self.chip, other))
            def _():
                self.chip_copy(other, self.chip).start()

    def collect(self):
        near = self.core == (0 if self.later else 1)
        self.local[...] = jnp.where(near, self.pair[...].astype(F32), 0.0)
        for other in range(self.chips):

            @pl.when(self.wanted(other, self.chip))
            def _():
                self.chip_copy(other, other).wait_recv()
                self.local[...] += self.arrived[other].astype(F32)

            @pl.when(self.wanted(self.chip, other))
            def _():
                self.chip_copy(other, self.chip).wait_send()


class SlabReduce:
    def __init__(self, ctx, me, chips, factor, left, tiles, kept, store, place, pair_in, chip_in, sems):
        self.chip, self.core = ctx // 2, lax.rem(ctx, 2)
        self.sibling = ctx + 1 - 2 * self.core
        self.me, self.chips, self.factor = me, chips, factor
        self.left, self.tiles, self.kept = left, tiles, kept
        self.store, self.place = store, place
        self.pair_in, self.chip_in, self.sems = pair_in, chip_in, sems

    def held(self, kind, p):
        slab = self.kept.shape[1]
        first = kind * self.chips * slab + p * slab
        return self.store.at[
            pl.ds(self.place, len(self.tiles)), pl.ds(pl.multiple_of(first, slab), slab), :
        ]

    def product(self, owner, put):
        _, slab, wide = self.kept.shape
        rows = self.left[pl.ds(pl.multiple_of(owner * slab, slab), slab), :]
        for tile, (right, base) in enumerate(self.tiles):
            put(tile, dot(rows, right[:, base : base + wide]) * self.factor)

    def pair_copy(self, p):
        return pltpu.make_async_remote_copy(
            src_ref=self.held(0, p), dst_ref=self.pair_in.at[p],
            send_sem=self.sems.at[0, p], recv_sem=self.sems.at[1, p],
            device_id=(self.sibling, self.me), device_id_type=MESH,
        )

    def chip_copy(self, target, origin):
        return pltpu.make_async_remote_copy(
            src_ref=self.held(1, target), dst_ref=self.chip_in.at[origin],
            send_sem=self.sems.at[2, target], recv_sem=self.sems.at[3, origin],
            device_id=(2 * target + self.core, self.me), device_id_type=MESH,
        )

    def to_pair(self, p):
        out = self.held(0, p)

        def put(tile, value):
            out[tile] = value.astype(BF16)

        self.product(2 * p + 1 - self.core, put)
        self.pair_copy(p).start()

    def to_chip(self, q):
        self.pair_copy(q).wait_recv()
        out = self.held(1, q)

        def put(tile, value):
            out[tile] = (value + self.pair_in[q, tile].astype(F32)).astype(BF16)

        self.product(2 * q + self.core, put)
        self.chip_copy(q, self.chip).start()

    def keep_own(self):
        self.pair_copy(self.chip).wait_recv()

        def put(tile, value):
            self.kept[tile] = value + self.pair_in[self.chip, tile].astype(F32)

        self.product(2 * self.chip + self.core, put)

    def collect(self):
        chips, chip = self.chips, self.chip

        @pl.loop(1, chips)
        def _(j):
            p = lax.rem(chip + chips - j, chips)
            self.chip_copy(p, p).wait_recv()
            self.kept[...] += self.chip_in[p].astype(F32)

    def finish(self):
        chips, chip = self.chips, self.chip

        @pl.loop(0, chips)
        def _(p):
            self.pair_copy(p).wait_send()

        @pl.loop(1, chips)
        def _(j):
            p = lax.rem(chip + j, chips)
            self.chip_copy(p, chip).wait_send()


class Share:
    def __init__(self, ctx, me, partner, chips, source, held, send, recv):
        self.ctx, self.me, self.partner, self.chips = ctx, me, partner, chips
        self.chip, self.core = ctx // 2, lax.rem(ctx, 2)
        self.source, self.held, self.send, self.recv = source, held, send, recv

    def at(self, ref, origin):
        rows = self.held.shape[0] // (2 * self.chips)
        return ref.at[pl.ds(pl.multiple_of(origin * rows, rows), rows), :]

    def copy(self, source, origin, sem, target):
        return pltpu.make_async_remote_copy(
            src_ref=self.at(source, origin), dst_ref=self.at(self.held, origin),
            send_sem=self.send.at[sem], recv_sem=self.recv.at[origin],
            device_id=target, device_id_type=MESH,
        )

    def inward(self):
        return self.copy(self.source, self.ctx, 0, (self.ctx, self.partner))

    def to_chip(self, p):
        return self.copy(self.held, self.ctx, 1 + p, (2 * p + self.core, self.me))

    def to_sibling(self, p):
        target = (self.ctx + 1 - 2 * self.core, self.me)
        return self.copy(self.held, 2 * p + self.core, 1 + self.chips + p, target)

    def arrival(self, origin):
        self.copy(self.held, origin, 0, (self.ctx, self.partner)).wait_recv()

    def spread(self):
        self.arrival(self.ctx)

        @pl.loop(1, self.chips)
        def _(j):
            self.to_chip(lax.rem(self.chip + j, self.chips)).start()

        self.to_sibling(self.chip).start()

    def hand_on(self):
        @pl.loop(1, self.chips)
        def _(j):
            p = lax.rem(self.chip + self.chips - j, self.chips)
            self.arrival(2 * p + self.core)
            self.to_sibling(p).start()

    def complete(self):
        @pl.loop(0, self.chips)
        def _(p):
            self.arrival(2 * p + 1 - self.core)

    def finish(self):
        @pl.loop(0, self.chips)
        def _(p):
            self.to_sibling(p).wait_send()

        @pl.loop(1, self.chips)
        def _(j):
            self.to_chip(lax.rem(self.chip + j, self.chips)).wait_send()


def run_slabs(parts, middle=None):
    chips, chip = parts[0].chips, parts[0].chip

    @pl.loop(1, chips + 1)
    def _(j):
        for part in parts:
            part.to_pair(lax.rem(chip + j, chips))

        @pl.when(j > 1)
        def _():
            for part in parts:
                part.to_chip(lax.rem(chip + j - 1, chips))


def block_kernel(
    n, chips, factor,
    x_hbm, cot_hbm, in_gain_ref, gain_ref, w_hbm, wo_hbm,
    outputs_ref, igrad_ref, qgrad_ref, ograd_ref,
    w_ref, wt_ref, wo_ref, wop_ref, load,
    normt_ref, proj_ref, mixed_ref, mixp_ref, gproj_ref,
    held_x, xsend, xrecv,
    held_c, cott_ref, csend, crecv,
    gm_ref, gsend, grecv, msend, mrecv, wsend, wrecv,
    total, po_ref, pi_ref, osend, orecv, og_ref, ogsem,
    back_out, back_in, bsend, brecv,
    scores, attended, gatt, gkey,
    local_f, mine_f, pair_f, sum_f, arrived_f, sems_f,
    local_b, mine_b, pair_b, sum_b, arrived_b, sems_b,
    q0, q1, qsems, k0, k1, ksems,
    kept_o, o0, o1, osems, kept_p, p0, p1, psems,
):
    ctx, me = lax.axis_index("ctx"), lax.axis_index("tp")
    rows = x_hbm.shape[0]
    block, width = mixed_ref.shape
    heads = width // DH
    chip, core = ctx // 2, lax.rem(ctx, 2)
    mate = me + 1 - 2 * lax.rem(me, 2)
    across = n - 1 - me
    beyond = n - 1 - mate
    edge = jnp.logical_or(me == 0, me == n - 1)
    inner = jnp.logical_not(edge)

    def row_at(origin):
        return pl.ds(pl.multiple_of(origin * rows, rows), rows)

    def cols(h, part=0):
        return pl.ds(pl.multiple_of(part * width + h * DH, DH), DH)

    def head_rows(h):
        return pl.ds(pl.multiple_of(h * DH, DH), DH)

    def causal(value):
        down = lax.broadcasted_iota(jnp.int32, (block, block), 0)
        along = lax.broadcasted_iota(jnp.int32, (block, block), 1)
        return jnp.where(down >= along, value, 0.0).astype(BF16)

    x_load = pltpu.make_async_copy(x_hbm, held_x.at[row_at(me), :], load.at[0])
    w_load = pltpu.make_async_copy(w_hbm, w_ref, load.at[1])
    c_load = pltpu.make_async_copy(cot_hbm, held_c.at[row_at(me), :], load.at[2])
    wo_load = pltpu.make_async_copy(wo_hbm, wo_ref, load.at[3])
    x_load.start()
    w_load.start()
    c_load.start()
    wo_load.start()
    others = [ctx + 1 - 2 * core]
    others += [2 * lax.rem(chip + j, chips) + core for j in range(1, chips)]
    line_barrier(ctx, me, n, others)
    gather_x = LineGather(ctx, me, n, x_hbm, held_x, xsend, xrecv)
    share = Share(ctx, me, mate, chips, wo_hbm, wop_ref, wsend, wrecv)
    forward = StateSum(ctx, me, chips, False, local_f, mine_f, pair_f, sum_f, arrived_f, sems_f)
    backward = StateSum(ctx, me, chips, True, local_b, mine_b, pair_b, sum_b, arrived_b, sems_b)
    reduce_q = SlabReduce(
        ctx, me, chips, factor, normt_ref, [(gproj_ref, 0)],
        qgrad_ref.at[0:1], w_ref, 0, q0, q1, qsems,
    )
    reduce_k = SlabReduce(
        ctx, me, chips, factor, normt_ref, [(gproj_ref, width), (gproj_ref, 2 * width)],
        qgrad_ref.at[1:3], w_ref, 1, k0, k1, ksems,
    )
    reduce_o = SlabReduce(
        ctx, me, chips, factor, cott_ref, [(mixed_ref, 0)], kept_o, w_ref, 1, o0, o1, osems
    )
    reduce_p = SlabReduce(
        ctx, me, chips, factor, cott_ref, [(mixp_ref, 0)], kept_p, w_ref, 2, p0, p1, psems
    )

    def remote(source, target, send, recv, device):
        return pltpu.make_async_remote_copy(
            src_ref=source, dst_ref=target, send_sem=send, recv_sem=recv,
            device_id=(ctx, device), device_id_type=MESH,
        )

    def cot_copy(source, origin, sem, device):
        return remote(
            source, held_c.at[row_at(origin), :], csend.at[sem], crecv.at[origin], device
        )

    def grad_copy(origin):
        piece = gm_ref.at[row_at(origin), :]
        return remote(piece, piece, gsend.at[origin], grecv.at[origin], mate)

    def mixed_copy(origin):
        at = row_at(origin)
        return remote(
            mixed_ref.at[at, :], mixp_ref.at[at, :], msend.at[origin], mrecv.at[origin], mate
        )

    def out_copy(slot, landing, device):
        return remote(
            po_ref.at[slot], pi_ref.at[landing], osend.at[slot], orecv.at[landing], device
        )

    def ograd_copy():
        return remote(og_ref, og_ref, ogsem.at[0], ogsem.at[1], mate)

    def project(source, origin):
        at = row_at(origin)
        piece = source[...].astype(F32)
        normed = (piece * row_scale(piece) * in_gain_ref[...]).astype(BF16)
        for part in range(3):
            here = slice(part * width, (part + 1) * width)
            proj_ref[at, here] = dot(normed, w_ref[part]).astype(BF16)
        normt_ref[:, at] = normed.T

    def turn_weight(first, last):
        step = 2 * DH
        count = w_ref.shape[1] // step

        @pl.loop(first, last)
        def _(k):
            part = k // count
            at = pl.ds(pl.multiple_of(lax.rem(k, count) * step, step), step)
            into = pl.ds(pl.multiple_of(part * width, width), width)
            wt_ref[into, at] = w_ref[part, at, :].T

    gather_x.start_up()
    gather_x.start_down()
    x_load.wait()
    w_load.wait()
    project(held_x.at[row_at(me), :], me)
    turns = 3 * w_ref.shape[1] // (2 * DH)
    turn_weight(0, turns // 2)

    @pl.loop(1, n)
    def _(d):
        gather_x.step(d)

        @pl.when(jnp.logical_and(edge, d == 1))
        def _():
            share.inward().start()
            cot_copy(cot_hbm, me, 0, mate).start()

        @pl.when(jnp.logical_and(inner, d == 2))
        def _():
            cot_copy(cot_hbm, me, 0, across).start()
            share.spread()

        @pl.when(me - d >= 0)
        def _():
            project(gather_x.at(me - d), me - d)

        @pl.when(me + d < n)
        def _():
            project(gather_x.at(me + d), me + d)

        @pl.when(d == 1)
        def _():
            turn_weight(turns // 2, turns)

    @pl.loop(0, heads)
    def _(h):
        local_f[head_rows(h), :] = dot(proj_ref[:, cols(h, 1)], proj_ref[:, cols(h, 2)], TN)

    forward.start()

    @pl.loop(0, heads)
    def _(h):
        scores[h] = causal(dot(proj_ref[:, cols(h)], proj_ref[:, cols(h, 1)], NT))

    forward.spread()

    @pl.loop(0, heads)
    def _(h):
        attended[:, cols(h)] = dot(scores[h], proj_ref[:, cols(h, 2)])

    forward.collect()

    @pl.loop(0, heads)
    def _(h):
        high, low = split(local_f[head_rows(h), :])
        query = proj_ref[:, cols(h)]
        value = attended[:, cols(h)] + dot(query, high) + dot(query, low)
        attended[:, cols(h)] = value
        mixed_ref[:, cols(h)] = (value * row_scale(value) * gain_ref[:, cols(h)]).astype(BF16)

    wo_load.wait()
    c_load.wait()

    def grad_rows(origin, value):
        at = row_at(origin)
        weighted = value * gain_ref[...]
        for h in range(heads):
            here = slice(h * DH, (h + 1) * DH)
            value = attended[at, here]
            scale = row_scale(value)
            part = weighted[:, here]
            mean = jnp.mean(part * value, axis=-1, keepdims=True)
            gatt[at, here] = (scale * part - scale * scale * scale * value * mean).astype(BF16)

    def own_rows(origin):
        grad_rows(origin, dot(held_c[row_at(origin), :], wo_ref[...], NT))

    def mate_rows(origin):
        at = row_at(origin)
        gm_ref[at, :] = dot(held_c[at, :], wop_ref[...], NT).astype(BF16)
        grad_copy(origin).start()

    def turn_cot(origin):
        at = row_at(origin)
        cott_ref[:, at] = held_c[at, :].T

    @pl.when(edge)
    def _():
        for origin in (across, beyond, mate, me):
            mixed_copy(origin).start()
        own_rows(me)
        for origin in (mate, beyond, across):
            grad_copy(origin).wait_recv()
            grad_rows(origin, gm_ref[row_at(origin), :].astype(F32))

    @pl.when(inner)
    def _():
        cot_copy(cot_hbm, mate, 0, mate).wait_recv()
        cot_copy(held_c.at[row_at(mate), :], mate, 1, across).start()
        share.hand_on()
        own_rows(me)
        own_rows(mate)
        share.complete()
        mate_rows(me)
        cot_copy(cot_hbm, across, 0, across).wait_recv()
        mate_rows(across)
        own_rows(across)
        turn_cot(me)
        turn_cot(mate)
        turn_cot(across)
        cot_copy(cot_hbm, beyond, 0, across).wait_recv()
        mate_rows(beyond)
        own_rows(beyond)

    @pl.loop(0, heads)
    def _(h):
        local_b[head_rows(h), :] = dot(proj_ref[:, cols(h)], gatt[:, cols(h)], TN)

    backward.start()

    @pl.when(inner)
    def _():
        turn_cot(beyond)

    backward.spread()

    @pl.when(inner)
    def _():
        run_slabs([reduce_o])

    @pl.loop(0, heads)
    def _(h):
        query, key = proj_ref[:, cols(h)], proj_ref[:, cols(h, 1)]
        grad = gatt[:, cols(h)]
        gscores = causal(dot(grad, proj_ref[:, cols(h, 2)], NT))
        high, low = split(local_f[head_rows(h), :])
        gquery = dot(gscores, key) + dot(grad, high, NT) + dot(grad, low, NT)
        gproj_ref[:, cols(h)] = gquery.astype(BF16)
        gkey[:, cols(h)] = dot(gscores, query, TN)

    def out_mine(origin, into):
        into[...] = dot(mixed_ref[row_at(origin), :], wo_ref[...])

    def out_both(origin, into):
        at = row_at(origin)
        into[...] = dot(mixed_ref[at, :], wo_ref[...])
        into[...] += dot(mixp_ref[at, :], wop_ref[...])

    @pl.when(inner)
    def _():
        for slot, origin in enumerate((beyond, across)):
            mixed_copy(origin).wait_recv()
            out_both(origin, total)
            po_ref[slot] = total[...].astype(BF16)
            out_copy(slot, slot, across).start()

    @pl.loop(0, heads)
    def _(h):
        attended[:, cols(h)] = dot(scores[h], gatt[:, cols(h)], TN)

    backward.collect()

    @pl.loop(0, heads)
    def _(h):
        high, low = split(local_b[head_rows(h), :])
        key, value = proj_ref[:, cols(h, 1)], proj_ref[:, cols(h, 2)]
        gk = gkey[:, cols(h)] + dot(value, high, NT) + dot(value, low, NT)
        gv = attended[:, cols(h)] + dot(key, high) + dot(key, low)
        gproj_ref[:, cols(h, 1)] = gk.astype(BF16)
        gproj_ref[:, cols(h, 2)] = gv.astype(BF16)

    def in_partial(t, into):
        into[...] = dot(gproj_ref[row_at(t), :], wt_ref[...])

    back = LineScatter(ctx, me, n, in_partial, total, back_out, back_in, bsend, brecv)
    back.step(0)

    @pl.when(inner)
    def _():
        mixed_copy(mate).wait_recv()
        mixed_copy(me).wait_recv()
        run_slabs([reduce_p])

    run_slabs([reduce_q])

    @pl.when(edge)
    def _():
        back.step(1)

    @pl.when(inner)
    def _():
        reduce_o.finish()
        reduce_p.finish()

    run_slabs([reduce_k])

    @pl.when(edge)
    def _():
        back.step(2)

    @pl.when(inner)
    def _():
        out_mine(mate, total)
        out_copy(0, 0, across).wait_recv()
        po_ref[2] = (total[...] + pi_ref[0].astype(F32)).astype(BF16)
        out_copy(2, 1, mate).start()
        back.step(1)
        reduce_o.keep_own()
        reduce_p.keep_own()
        reduce_o.collect()
        reduce_p.collect()
        og_ref[...] = kept_p[0].astype(BF16)
        ograd_copy().start()
        ograd_ref[...] = kept_o[0]
        out_both(me, total)
        out_copy(1, 1, across).wait_recv()
        outputs_ref[...] = (
            held_x[row_at(me), :].astype(F32) + total[...] + pi_ref[1].astype(F32)
        ).astype(BF16)

    reduce_q.keep_own()
    reduce_k.keep_own()

    @pl.when(inner)
    def _():
        back.step(2)

    @pl.when(edge)
    def _():
        out_mine(me, total)
        out_copy(2, 1, mate).wait_recv()
        outputs_ref[...] = (
            held_x[row_at(me), :].astype(F32) + total[...] + pi_ref[1].astype(F32)
        ).astype(BF16)
        ograd_copy().wait_recv()
        ograd_ref[...] = og_ref[...].astype(F32)

    reduce_q.collect()
    reduce_k.collect()
    back.finish()
    piece = held_x[row_at(me), :].astype(F32)
    scale = row_scale(piece)
    weighted = total[...] * in_gain_ref[...]
    mean = jnp.mean(weighted * piece, axis=-1, keepdims=True)
    igrad_ref[...] = (
        held_c[row_at(me), :].astype(F32) + scale * weighted - scale * scale * scale * piece * mean
    ).astype(BF16)
    gather_x.finish()
    reduce_q.finish()
    reduce_k.finish()

    @pl.when(edge)
    def _():
        share.inward().wait_send()
        cot_copy(cot_hbm, me, 0, mate).wait_send()
        for origin in (across, beyond, mate, me):
            mixed_copy(origin).wait_send()

    @pl.when(inner)
    def _():
        share.finish()
        cot_copy(cot_hbm, me, 0, across).wait_send()
        cot_copy(held_c.at[row_at(mate), :], mate, 1, across).wait_send()
        for origin in (me, across, beyond):
            grad_copy(origin).wait_send()
        out_copy(0, 0, across).wait_send()
        out_copy(1, 1, across).wait_send()
        out_copy(2, 1, mate).wait_send()
        ograd_copy().wait_send()


def vmem(*shape, dtype=BF16):
    return pltpu.VMEM(shape, dtype)


def shards(inputs, norm_gain, qkv_weight, head_gain, out_weight, out_cotangent):
    rows, width = inputs.shape
    local_width = qkv_weight.shape[2]
    heads = local_width // DH
    n = lax.axis_size("tp")
    ctx_size = lax.axis_size("ctx")
    chips = ctx_size // 2
    block = rows * n
    slab = width // ctx_size
    factor = 1.0 / math.sqrt(block * ctx_size)
    dma = pltpu.SemaphoreType.DMA
    shape = jax.ShapeDtypeStruct
    state = [
        vmem(heads * DH, DH, dtype=F32),
        vmem(heads * DH, DH),
        vmem(heads * DH, DH),
        vmem(heads * DH, DH),
        vmem(chips, heads * DH, DH),
        dma((2, chips + 1)),
    ]

    def slabs(tiles):
        return [vmem(chips, tiles, slab, local_width)] * 2 + [dma((4, chips))]

    kept = [vmem(1, slab, local_width, dtype=F32)]
    scratch = (
        [vmem(3, width, local_width), vmem(3 * local_width, width)]
        + [vmem(local_width, width)] * 2
        + [dma((4,))]
        + [vmem(width, block), vmem(block, 3 * local_width)]
        + [vmem(block, local_width)] * 2
        + [vmem(block, 3 * local_width)]
        + [vmem(block, width), dma((2, n)), dma((n,))]
        + [vmem(block, width), vmem(width, block), dma((2,)), dma((n,))]
        + [vmem(block, local_width), dma((n,)), dma((n,)), dma((n,)), dma((n,))]
        + [dma((1 + 2 * chips,)), dma((ctx_size,))]
        + [vmem(rows, width, dtype=F32), vmem(3, rows, width), vmem(2, rows, width)]
        + [dma((3,)), dma((2,)), vmem(slab, local_width), dma((2,))]
        + [vmem(n, rows, width), vmem(n + 1, rows, width), dma((n,)), dma((n + 1,))]
        + [vmem(heads, block, block), vmem(block, local_width, dtype=F32)]
        + [vmem(block, local_width), vmem(block, local_width, dtype=F32)]
        + state
        + state
        + slabs(1)
        + slabs(2)
        + kept
        + slabs(1)
        + kept
        + slabs(1)
    )
    held = pl.BlockSpec(memory_space=pltpu.VMEM)
    anywhere = pl.BlockSpec(memory_space=pl.ANY)
    outputs, input_grad, qkv_grad, out_grad_t = pl.pallas_call(
        functools.partial(block_kernel, n, chips, factor),
        name="block",
        out_shape=[
            shape((rows, width), BF16),
            shape((rows, width), BF16),
            shape((3, slab, local_width), F32),
            shape((slab, local_width), F32),
        ],
        in_specs=[anywhere] * 2 + [held] * 2 + [anywhere] * 2,
        out_specs=[held] * 4,
        scratch_shapes=scratch,
        compiler_params=pltpu.CompilerParams(
            collective_id=0, has_side_effects=True, vmem_limit_bytes=VMEM_LIMIT
        ),
    )(
        inputs,
        out_cotangent,
        norm_gain.reshape(1, width),
        head_gain.reshape(1, local_width),
        qkv_weight.transpose(1, 0, 2),
        out_weight,
    )
    return (outputs, input_grad, qkv_grad.transpose(1, 0, 2), out_grad_t)


def solution(mesh):
    in_specs = (
        P(("ctx", "tp"), None),
        P(),
        P(None, None, "tp"),
        P("tp"),
        P("tp", None),
        P(("ctx", "tp"), None),
    )
    out_specs = (
        P(("ctx", "tp"), None),
        P(("ctx", "tp"), None),
        P("ctx", None, "tp"),
        P("ctx", "tp"),
    )
    return jax.shard_map(shards, mesh=mesh, in_specs=in_specs, out_specs=out_specs, check_vma=False)
```

```python
import functools
import math

import jax
import jax.numpy as jnp
from jax import lax
from jax.experimental import pallas as pl
from jax.experimental.pallas import tpu as pltpu
from jax.sharding import PartitionSpec as P

DH = 128
EPSILON = 1e-05
MESH = pl.DeviceIdType.MESH
F32 = jnp.float32
BF16 = jnp.bfloat16
VMEM_LIMIT = 63 * 1024 * 1024
NN = (((1,), (0,)), ((), ()))
NT = (((1,), (1,)), ((), ()))
TN = (((0,), (0,)), ((), ()))


def dot(a, b, dims=NN):
    return lax.dot_general(a, b, dims, preferred_element_type=F32)


def row_scale(rows):
    return lax.rsqrt(jnp.mean(rows * rows, axis=-1, keepdims=True) + EPSILON)


def split(value):
    high = value.astype(BF16)
    return high, (value - high.astype(F32)).astype(BF16)


def line_barrier(ctx, me, n, others):
    barrier = pltpu.get_barrier_semaphore()

    @pl.when(me > 0)
    def _():
        pl.semaphore_signal(barrier, inc=1, device_id=(ctx, me - 1), device_id_type=MESH)

    @pl.when(me < n - 1)
    def _():
        pl.semaphore_signal(barrier, inc=1, device_id=(ctx, me + 1), device_id_type=MESH)

    for other in others:
        pl.semaphore_signal(barrier, inc=1, device_id=(other, me), device_id_type=MESH)
    inner = jnp.logical_and(me > 0, me < n - 1)

    @pl.when(inner)
    def _():
        pl.semaphore_wait(barrier, 2 + len(others))

    @pl.when(jnp.logical_not(inner))
    def _():
        pl.semaphore_wait(barrier, 1 + len(others))


class LineGather:
    def __init__(self, ctx, me, n, own, held, send, recv):
        self.ctx, self.me, self.n = ctx, me, n
        self.own, self.held, self.send, self.recv = own, held, send, recv

    def at(self, origin):
        rows = self.own.shape[0]
        return self.held.at[pl.ds(pl.multiple_of(origin * rows, rows), rows), :]

    def copy(self, source, origin, up):
        target = self.me + 1 if up else self.me - 1
        return pltpu.make_async_remote_copy(
            src_ref=source,
            dst_ref=self.at(origin),
            send_sem=self.send.at[1 if up else 0, origin],
            recv_sem=self.recv.at[origin],
            device_id=(self.ctx, target),
            device_id_type=MESH,
        )

    def start_up(self):
        @pl.when(self.me < self.n - 1)
        def _():
            self.copy(self.own, self.me, True).start()

    def start_down(self):
        @pl.when(self.me > 0)
        def _():
            self.copy(self.own, self.me, False).start()

    def step(self, d):
        below, above = self.me - d, self.me + d

        @pl.when(below >= 0)
        def _():
            self.copy(self.at(below), below, True).wait_recv()

            @pl.when(self.me < self.n - 1)
            def _():
                self.copy(self.at(below), below, True).start()

        @pl.when(above < self.n)
        def _():
            self.copy(self.at(above), above, False).wait_recv()

            @pl.when(self.me > 0)
            def _():
                self.copy(self.at(above), above, False).start()

    def finish(self):
        for origin in range(self.n):

            @pl.when(jnp.logical_and(origin <= self.me, self.me < self.n - 1))
            def _():
                self.copy(self.at(origin), origin, True).wait_send()

            @pl.when(jnp.logical_and(origin >= self.me, self.me > 0))
            def _():
                self.copy(self.at(origin), origin, False).wait_send()


class LineScatter:
    def __init__(self, ctx, me, n, partial, total, out, arrived, send, recv):
        self.ctx, self.me, self.n = ctx, me, n
        self.partial, self.total, self.out = partial, total, out
        self.arrived = arrived
        self.send, self.recv = send, recv

    def copy(self, t, up, slot):
        target = self.me + 1 if up else self.me - 1
        return pltpu.make_async_remote_copy(
            src_ref=self.out.at[t],
            dst_ref=self.arrived.at[slot],
            send_sem=self.send.at[t],
            recv_sem=self.recv.at[slot],
            device_id=(self.ctx, target),
            device_id_type=MESH,
        )

    def add(self, slot):
        self.copy(0, True, slot).wait_recv()
        self.total[...] += self.arrived[slot].astype(F32)

    def step(self, s):
        me, n = self.me, self.n

        @pl.when(s >= me)
        def _():
            t = n - 1 - s + me
            self.partial(t, self.total)

            @pl.when(me > 0)
            def _():
                self.add(t)

            self.out[t] = self.total[...].astype(BF16)
            self.copy(t, True, t).start()

        @pl.when(s >= n - 1 - me)
        def _():
            t = s - (n - 1 - me)
            self.partial(t, self.total)

            @pl.when(me < n - 1)
            def _():
                self.add(t)

            self.out[t] = self.total[...].astype(BF16)
            self.copy(t, False, n if s == n - 2 else t).start()

    def finish(self):
        me, n = self.me, self.n
        self.partial(me, self.total)

        @pl.when(me > 0)
        def _():
            self.add(me)

        @pl.when(me < n - 1)
        def _():
            self.add(n)

        for t in range(n):

            @pl.when(t != me)
            def _():
                self.copy(t, True, t).wait_send()


class StateSum:
    def __init__(self, ctx, me, chips, later, local, mine, pair, chip_sum, arrived, sems, turns):
        self.chip, self.core = ctx // 2, lax.rem(ctx, 2)
        self.sibling = ctx + 1 - 2 * self.core
        self.me, self.chips, self.later = me, chips, later
        self.local, self.mine, self.pair = local, mine, pair
        self.chip_sum, self.arrived = chip_sum, arrived
        self.sems, self.turns = sems, turns
        half = chip_sum.shape[0]
        self.half = pl.ds(pl.multiple_of(self.core * half, half), half)

    def pair_copy(self):
        return pltpu.make_async_remote_copy(
            src_ref=self.mine,
            dst_ref=self.pair,
            send_sem=self.sems.at[0, 0],
            recv_sem=self.sems.at[1, 0],
            device_id=(self.sibling, self.me),
            device_id_type=MESH,
        )

    def chip_copy(self, target, origin):
        return pltpu.make_async_remote_copy(
            src_ref=self.chip_sum,
            dst_ref=self.arrived.at[origin, self.half, :],
            send_sem=self.sems.at[0, target + 1],
            recv_sem=self.sems.at[1, origin + 1],
            device_id=(2 * target + self.core, self.me),
            device_id_type=MESH,
        )

    def core_copy(self, origin):
        piece = self.arrived.at[origin, self.half, :]
        return pltpu.make_async_remote_copy(
            src_ref=piece,
            dst_ref=piece,
            send_sem=self.turns.at[0, origin],
            recv_sem=self.turns.at[1, origin],
            device_id=(self.sibling, self.me),
            device_id_type=MESH,
        )

    def wanted(self, source, target):
        return source > target if self.later else source < target

    def start(self):
        self.mine[...] = self.local[...].astype(BF16)
        self.pair_copy().start()

    def spread(self):
        self.pair_copy().wait()
        own = self.local[self.half, :] + self.pair[self.half, :].astype(F32)
        self.chip_sum[...] = own.astype(BF16)
        for other in range(self.chips):

            @pl.when(self.wanted(self.chip, other))
            def _():
                self.chip_copy(other, self.chip).start()

    def hand_on(self):
        for other in range(self.chips):

            @pl.when(self.wanted(other, self.chip))
            def _():
                self.chip_copy(other, other).wait_recv()
                self.core_copy(other).start()

    def collect(self):
        near = self.core == (0 if self.later else 1)
        self.local[...] = jnp.where(near, self.pair[...].astype(F32), 0.0)
        for other in range(self.chips):

            @pl.when(self.wanted(other, self.chip))
            def _():
                self.core_copy(other).wait_recv()
                self.local[...] += self.arrived[other].astype(F32)

    def finish(self):
        for other in range(self.chips):

            @pl.when(self.wanted(other, self.chip))
            def _():
                self.core_copy(other).wait_send()

            @pl.when(self.wanted(self.chip, other))
            def _():
                self.chip_copy(other, self.chip).wait_send()


class SlabReduce:
    def __init__(self, ctx, me, chips, factor, left, parts, kept, stores, arrivals, sems):
        self.chip, self.core = ctx // 2, lax.rem(ctx, 2)
        self.sibling = ctx + 1 - 2 * self.core
        self.me, self.chips, self.factor = me, chips, factor
        self.left, self.parts, self.kept, self.stores = left, parts, kept, stores
        self.pair_in, self.near_in, self.far_in = arrivals
        self.pair_sems, self.near_sems, self.far_sems = sems
        self.m = self.near_in.shape[1] + 1
        self.slab, self.wide = self.far_in.shape[2:]
        low, high = lax.rem(self.chip, self.m), self.chip // self.m
        self.first, self.second = (low, high), (high, low)

    def chip_of(self, side, first, second):
        return second * self.m + first if side == 0 else first * self.m + second

    def held(self, side, start, size):
        ref, column = self.stores[side]
        depth = ref.shape[0]
        row = pl.multiple_of(lax.rem(start, depth), size)
        column = pl.multiple_of(start // depth * 2 * self.wide + column, self.wide)
        return ref.at[pl.ds(row, size), pl.ds(column, self.wide)]

    def near_out(self, side, j):
        size = self.m * self.slab
        return self.held(side, self.chips * self.slab + (j - 1) * size, size)

    def far_out(self, side, j):
        start = (self.chips + self.m * (self.m - 1) + j - 1) * self.slab
        return self.held(side, start, self.slab)

    def times(self, rows, side):
        right, base = self.parts[side]
        return dot(rows, right[:, base : base + self.wide]) * self.factor

    def one_slab(self, side, second):
        first = self.first[side]
        high, low = (second, first) if side == 0 else (first, second)
        value = self.times(self.left[high, low, self.core], side)
        at = pl.ds(pl.multiple_of(low * self.slab, self.slab), self.slab)
        value = value + self.pair_in[side, high, at, :].astype(F32)
        row = pl.multiple_of(second * self.slab, self.slab)
        for j in range(1, self.m):
            value = value + self.near_in[side, j - 1, pl.ds(row, self.slab), :].astype(F32)
        return value

    def pair_copy(self, side, k):
        size = self.m * self.slab
        return pltpu.make_async_remote_copy(
            src_ref=self.held(side, k * size, size),
            dst_ref=self.pair_in.at[side, k],
            send_sem=self.pair_sems.at[0, side, k],
            recv_sem=self.pair_sems.at[1, side, k],
            device_id=(self.sibling, self.me), device_id_type=MESH,
        )

    def near_copy(self, side, j):
        first = lax.rem(self.first[side] + j, self.m)
        target = self.chip_of(side, first, self.second[side])
        return pltpu.make_async_remote_copy(
            src_ref=self.near_out(side, j), dst_ref=self.near_in.at[side, j - 1],
            send_sem=self.near_sems.at[0, side, j], recv_sem=self.near_sems.at[1, side, j],
            device_id=(2 * target + self.core, self.me), device_id_type=MESH,
        )

    def far_copy(self, side, j):
        second = lax.rem(self.second[side] + j, self.m)
        target = self.chip_of(side, self.first[side], second)
        return pltpu.make_async_remote_copy(
            src_ref=self.far_out(side, j), dst_ref=self.far_in.at[side, j - 1],
            send_sem=self.far_sems.at[0, side, j], recv_sem=self.far_sems.at[1, side, j],
            device_id=(2 * target + self.core, self.me), device_id_type=MESH,
        )

    def to_pair(self):
        size = self.m * self.slab

        @pl.loop(0, self.m)
        def _(k):
            rows = self.left[k, :, 1 - self.core]
            rows = rows.reshape(size, rows.shape[-1])
            for side in range(2):
                self.held(side, k * size, size)[...] = self.times(rows, side).astype(BF16)
                self.pair_copy(side, k).start()

    def to_near(self):
        for side in range(2):
            @pl.loop(0, self.m)
            def _(k):
                self.pair_copy(side, k).wait_recv()

            @pl.loop(1, self.m)
            def _(j):
                first = lax.rem(self.first[side] + j, self.m)
                first_rows = pl.ds(pl.multiple_of(first * self.slab, self.slab), self.slab)
                if side == 0:
                    rows, pair = self.left[:, first, self.core], self.pair_in[side, :, first_rows]
                else:
                    rows, pair = self.left[first, :, self.core], self.pair_in[side, first]
                size = self.m * self.slab
                value = self.times(rows.reshape(size, rows.shape[-1]), side)
                value = value + pair.reshape(size, self.wide).astype(F32)
                self.near_out(side, j)[...] = value.astype(BF16)
                self.near_copy(side, j).start()

    def to_far(self):
        for side in range(2):

            @pl.loop(1, self.m)
            def _(j):
                self.near_copy(side, j).wait_recv()

            @pl.loop(1, self.m)
            def _(j):
                second = lax.rem(self.second[side] + j, self.m)
                self.far_out(side, j)[...] = self.one_slab(side, second).astype(BF16)
                self.far_copy(side, j).start()

    def keep_own(self):
        for side in range(2):
            ref, column = self.kept[side]
            ref[:, column : column + self.wide] = self.one_slab(side, self.second[side])

    def collect(self):
        for side in range(2):
            ref, column = self.kept[side]

            @pl.loop(1, self.m)
            def _(j):
                self.far_copy(side, j).wait_recv()
                ref[:, column : column + self.wide] += self.far_in[side, j - 1].astype(F32)

    def finish(self):
        for side in range(2):

            @pl.loop(0, self.m)
            def _(k):
                self.pair_copy(side, k).wait_send()

            @pl.loop(1, self.m)
            def _(j):
                self.near_copy(side, j).wait_send()
                self.far_copy(side, j).wait_send()


class Share:
    def __init__(self, ctx, me, partner, chips, source, held, send, recv):
        self.ctx, self.me, self.partner, self.chips = ctx, me, partner, chips
        self.chip, self.core = ctx // 2, lax.rem(ctx, 2)
        self.source, self.held, self.send, self.recv = source, held, send, recv

    def at(self, ref, origin):
        rows = self.held.shape[0] // (2 * self.chips)
        return ref.at[pl.ds(pl.multiple_of(origin * rows, rows), rows), :]

    def copy(self, source, origin, sem, target):
        return pltpu.make_async_remote_copy(
            src_ref=self.at(source, origin), dst_ref=self.at(self.held, origin),
            send_sem=self.send.at[sem], recv_sem=self.recv.at[origin],
            device_id=target, device_id_type=MESH,
        )

    def inward(self):
        return self.copy(self.source, self.ctx, 0, (self.ctx, self.partner))

    def to_chip(self, p):
        return self.copy(self.held, self.ctx, 1 + p, (2 * p + self.core, self.me))

    def to_sibling(self, p):
        target = (self.ctx + 1 - 2 * self.core, self.me)
        return self.copy(self.held, 2 * p + self.core, 1 + self.chips + p, target)

    def arrival(self, origin):
        self.copy(self.held, origin, 0, (self.ctx, self.partner)).wait_recv()

    def spread(self):
        self.arrival(self.ctx)

        @pl.loop(1, self.chips)
        def _(j):
            self.to_chip(lax.rem(self.chip + j, self.chips)).start()

        self.to_sibling(self.chip).start()

    def hand_on(self):
        @pl.loop(1, self.chips)
        def _(j):
            p = lax.rem(self.chip + self.chips - j, self.chips)
            self.arrival(2 * p + self.core)
            self.to_sibling(p).start()

    def complete(self):
        @pl.loop(0, self.chips)
        def _(p):
            self.arrival(2 * p + 1 - self.core)

    def finish(self):
        @pl.loop(0, self.chips)
        def _(p):
            self.to_sibling(p).wait_send()

        @pl.loop(1, self.chips)
        def _(j):
            self.to_chip(lax.rem(self.chip + j, self.chips)).wait_send()


def block_kernel(
    n, chips, factor,
    x_hbm, cot_hbm, in_gain_ref, gain_ref, w_hbm, wo_hbm,
    outputs_hbm, igrad_hbm, qgrad_hbm, ograd_hbm,
    outputs_ref, igrad_ref, qgrad_ref, ograd_ref,
    w_ref, wt_ref, both_wo, load,
    normt_ref, proj_ref, both_mixed, gproj_ref,
    x_ref, held_x, xsend, xrecv,
    held_c, cott_ref, csend, crecv,
    gm_ref, gsend, grecv, msend, mrecv, wsend, wrecv,
    total, po_ref, pi_ref, osend, orecv, og_ref, ogsem,
    back_out, back_in, bsend, brecv,
    scores, attended, gatt, gkey,
    local_f, mine_f, pair_f, sum_f, arrived_f, sems_f, turns_f,
    local_b, mine_b, pair_b, sum_b, arrived_b, sems_b, turns_b,
    q0, q1, q2, q3, q4, q5, k0, k1, k2, k3, k4, k5,
    kept_p, o0, o1, o2, o3, o4, o5, p0, p1, p2, p3, p4, p5,
):
    ctx, me = lax.axis_index("ctx"), lax.axis_index("tp")
    rows = x_hbm.shape[0]
    block, width = both_mixed.shape[0], both_mixed.shape[1] // 2
    mixed_ref, mixp_ref = both_mixed.at[:, :width], both_mixed.at[:, width:]
    wo_ref, wop_ref = both_wo.at[:width], both_wo.at[width:]
    heads = width // DH
    chip, core = ctx // 2, lax.rem(ctx, 2)
    mate = me + 1 - 2 * lax.rem(me, 2)
    across = n - 1 - me
    beyond = n - 1 - mate
    edge = jnp.logical_or(me == 0, me == n - 1)
    inner = jnp.logical_not(edge)

    def store(source, target, sem):
        copy = pltpu.make_async_copy(source, target, load.at[sem])
        copy.start()
        return copy

    def row_at(origin):
        return pl.ds(pl.multiple_of(origin * rows, rows), rows)

    def cols(h, part=0):
        return pl.ds(pl.multiple_of(part * width + h * DH, DH), DH)

    def head_rows(h):
        return pl.ds(pl.multiple_of(h * DH, DH), DH)

    def causal(value):
        down = lax.broadcasted_iota(jnp.int32, (block, block), 0)
        along = lax.broadcasted_iota(jnp.int32, (block, block), 1)
        return jnp.where(down >= along, value, 0.0).astype(BF16)

    x_load = pltpu.make_async_copy(x_hbm, x_ref, load.at[0])
    w_load = pltpu.make_async_copy(w_hbm, w_ref, load.at[1])
    c_load = pltpu.make_async_copy(cot_hbm, held_c.at[row_at(me), :], load.at[2])
    wo_load = pltpu.make_async_copy(wo_hbm, wo_ref, load.at[3])
    x_load.start()
    w_load.start()
    c_load.start()
    wo_load.start()
    others = [ctx + 1 - 2 * core]
    others += [2 * lax.rem(chip + j, chips) + core for j in range(1, chips)]
    line_barrier(ctx, me, n, others)
    gather_x = LineGather(ctx, me, n, x_hbm, held_x, xsend, xrecv)
    share = Share(ctx, me, mate, chips, wo_hbm, wop_ref, wsend, wrecv)
    forward = StateSum(
        ctx, me, chips, False, local_f, mine_f, pair_f, sum_f, arrived_f, sems_f, turns_f
    )
    backward = StateSum(
        ctx, me, chips, True, local_b, mine_b, pair_b, sum_b, arrived_b, sems_b, turns_b
    )
    half = width // 2
    reduce_q = SlabReduce(
        ctx, me, chips, factor, normt_ref, [(gproj_ref, 0), (gproj_ref, half)],
        [(qgrad_ref.at[0], 0), (qgrad_ref.at[0], half)],
        [(w_ref.at[0], 0), (w_ref.at[0], half)], (q0, q1, q2), (q3, q4, q5),
    )
    reduce_k = SlabReduce(
        ctx, me, chips, factor, normt_ref, [(gproj_ref, width), (gproj_ref, 2 * width)],
        [(qgrad_ref.at[1], 0), (qgrad_ref.at[2], 0)],
        [(w_ref.at[1], 0), (w_ref.at[2], 0)], (k0, k1, k2), (k3, k4, k5),
    )
    reduce_o = SlabReduce(
        ctx, me, chips, factor, cott_ref, [(mixed_ref, 0), (mixed_ref, half)],
        [(ograd_ref, 0), (ograd_ref, half)],
        [(w_ref.at[1], 0), (w_ref.at[1], half)], (o0, o1, o2), (o3, o4, o5),
    )
    reduce_p = SlabReduce(
        ctx, me, chips, factor, cott_ref, [(mixp_ref, 0), (mixp_ref, half)],
        [(kept_p, 0), (kept_p, half)],
        [(held_x, 0), (held_x, half)], (p0, p1, p2), (p3, p4, p5),
    )

    def remote(source, target, send, recv, device):
        return pltpu.make_async_remote_copy(
            src_ref=source, dst_ref=target, send_sem=send, recv_sem=recv,
            device_id=(ctx, device), device_id_type=MESH,
        )

    def cot_copy(source, origin, sem, device):
        return remote(
            source, held_c.at[row_at(origin), :], csend.at[sem], crecv.at[origin], device
        )

    def grad_copy(origin):
        piece = gm_ref.at[row_at(origin), :]
        return remote(piece, piece, gsend.at[origin], grecv.at[origin], mate)

    def mixed_copy(origin):
        at = row_at(origin)
        return remote(
            mixed_ref.at[at, :], mixp_ref.at[at, :], msend.at[origin], mrecv.at[origin], mate
        )

    def out_copy(slot, landing, device):
        return remote(
            po_ref.at[slot], pi_ref.at[landing], osend.at[slot], orecv.at[landing], device
        )

    def ograd_copy():
        return remote(og_ref, og_ref, ogsem.at[0], ogsem.at[1], mate)

    def project(source, origin):
        at = row_at(origin)
        piece = source[...].astype(F32)
        normed = (piece * row_scale(piece) * in_gain_ref[...]).astype(BF16)
        for part in range(3):
            here = slice(part * width, (part + 1) * width)
            proj_ref[at, here] = dot(normed, w_ref[part]).astype(BF16)
        normt_ref[:, :, :, :, at] = normed.T.reshape(normt_ref.shape[:4] + (rows,))

    def turn_weight(first, last):
        step = 2 * DH
        count = w_ref.shape[1] // step

        @pl.loop(first, last)
        def _(k):
            part = k // count
            at = pl.ds(pl.multiple_of(lax.rem(k, count) * step, step), step)
            into = pl.ds(pl.multiple_of(part * width, width), width)
            wt_ref[into, at] = w_ref[part, at, :].T

    gather_x.start_up()
    gather_x.start_down()
    x_load.wait()
    w_load.wait()
    project(x_ref, me)
    turns = 3 * w_ref.shape[1] // (2 * DH)
    turn_weight(0, turns // 2)

    @pl.loop(1, n)
    def _(d):
        @pl.when(jnp.logical_and(inner, d == 2))
        def _():
            share.spread()

        gather_x.step(d)

        @pl.when(jnp.logical_and(edge, d == 1))
        def _():
            share.inward().start()

        @pl.when(d == 2)
        def _():
            cot_copy(cot_hbm, me, 0, jnp.where(edge, mate, across)).start()

        @pl.when(me - d >= 0)
        def _():
            project(gather_x.at(me - d), me - d)

        @pl.when(me + d < n)
        def _():
            project(gather_x.at(me + d), me + d)

        @pl.when(d == 1)
        def _():
            turn_weight(turns // 2, turns)

    @pl.loop(0, heads)
    def _(h):
        local_f[head_rows(h), :] = dot(proj_ref[:, cols(h, 1)], proj_ref[:, cols(h, 2)], TN)

    forward.start()

    @pl.loop(0, heads)
    def _(h):
        scores[h] = causal(dot(proj_ref[:, cols(h)], proj_ref[:, cols(h, 1)], NT))

    forward.spread()

    @pl.loop(0, heads)
    def _(h):
        attended[:, cols(h)] = dot(scores[h], proj_ref[:, cols(h, 2)])

    forward.hand_on()

    @pl.when(inner)
    def _():
        share.hand_on()

    forward.collect()

    @pl.loop(0, heads)
    def _(h):
        high, low = split(local_f[head_rows(h), :])
        query = proj_ref[:, cols(h)]
        value = attended[:, cols(h)] + dot(query, high) + dot(query, low)
        attended[:, cols(h)] = value
        mixed_ref[:, cols(h)] = (value * row_scale(value) * gain_ref[:, cols(h)]).astype(BF16)

    wo_load.wait()
    c_load.wait()

    def grad_rows(at, value):
        weighted = value * gain_ref[...]
        for h in range(heads):
            here = slice(h * DH, (h + 1) * DH)
            value = attended[at, here]
            scale = row_scale(value)
            part = weighted[:, here]
            mean = jnp.mean(part * value, axis=-1, keepdims=True)
            gatt[at, here] = (scale * part - scale * scale * scale * value * mean).astype(BF16)

    def rows_from(origin, count=1):
        return pl.ds(pl.multiple_of(origin * rows, rows), count * rows)

    def own_rows(origin, count=1):
        at = rows_from(origin, count)
        grad_rows(at, dot(held_c[at, :], wo_ref[...], NT))

    def mate_rows(origin, count=1):
        at = rows_from(origin, count)
        gm_ref[at, :] = dot(held_c[at, :], wop_ref[...], NT).astype(BF16)
        for k in range(count):
            grad_copy(origin + k).start()

    def turn_cot(origin):
        at = row_at(origin)
        cott_ref[:, :, :, :, at] = held_c[at, :].T.reshape(cott_ref.shape[:4] + (rows,))

    @pl.when(edge)
    def _():
        for origin in (across, beyond, mate, me):
            mixed_copy(origin).start()
        own_rows(me)
        for origin in (mate, beyond, across):
            grad_copy(origin).wait_recv()
            grad_rows(row_at(origin), gm_ref[row_at(origin), :].astype(F32))

    @pl.when(inner)
    def _():
        cot_copy(cot_hbm, mate, 0, mate).wait_recv()
        cot_copy(held_c.at[row_at(mate), :], mate, 1, across).start()
        share.complete()
        cot_copy(cot_hbm, across, 0, across).wait_recv()
        mate_rows(1, n - 2)
        own_rows(me - 1, n - 1)
        turn_cot(me)
        turn_cot(mate)
        turn_cot(across)
        cot_copy(cot_hbm, beyond, 0, across).wait_recv()
        mate_rows(beyond)
        own_rows(beyond)

    @pl.loop(0, heads)
    def _(h):
        local_b[head_rows(h), :] = dot(proj_ref[:, cols(h)], gatt[:, cols(h)], TN)

    backward.start()

    @pl.when(inner)
    def _():
        turn_cot(beyond)
        reduce_o.to_pair()

    backward.spread()

    @pl.when(inner)
    def _():
        reduce_o.to_near()

    @pl.loop(0, heads)
    def _(h):
        query, key = proj_ref[:, cols(h)], proj_ref[:, cols(h, 1)]
        grad = gatt[:, cols(h)]
        gscores = causal(dot(grad, proj_ref[:, cols(h, 2)], NT))
        high, low = split(local_f[head_rows(h), :])
        gquery = dot(gscores, key) + dot(grad, high, NT) + dot(grad, low, NT)
        gproj_ref[:, cols(h)] = gquery.astype(BF16)
        gkey[:, cols(h)] = dot(gscores, query, TN)

    def out_mine(origin, into):
        into[...] = dot(mixed_ref[row_at(origin), :], wo_ref[...])

    def out_both(origin, into):
        into[...] = dot(both_mixed[row_at(origin), :], both_wo[...])

    backward.hand_on()
    gather_x.finish()

    @pl.when(inner)
    def _():
        for slot, origin in enumerate((beyond, across)):
            mixed_copy(origin).wait_recv()
            out_both(origin, total)
            po_ref[slot] = total[...].astype(BF16)
            out_copy(slot, slot, across).start()
        mixed_copy(mate).wait_recv()
        mixed_copy(me).wait_recv()
        reduce_p.to_pair()
        reduce_o.to_far()
        reduce_p.to_near()

    @pl.loop(0, heads)
    def _(h):
        attended[:, cols(h)] = dot(scores[h], gatt[:, cols(h)], TN)

    backward.collect()

    @pl.loop(0, heads)
    def _(h):
        high, low = split(local_b[head_rows(h), :])
        key, value = proj_ref[:, cols(h, 1)], proj_ref[:, cols(h, 2)]
        gk = gkey[:, cols(h)] + dot(value, high, NT) + dot(value, low, NT)
        gv = attended[:, cols(h)] + dot(key, high) + dot(key, low)
        gproj_ref[:, cols(h, 1)] = gk.astype(BF16)
        gproj_ref[:, cols(h, 2)] = gv.astype(BF16)

    def in_partial(t, into):
        into[...] = dot(gproj_ref[row_at(t), :], wt_ref[...])

    back = LineScatter(ctx, me, n, in_partial, total, back_out, back_in, bsend, brecv)
    back.step(0)
    reduce_q.to_pair()
    reduce_q.to_near()

    @pl.when(inner)
    def _():
        reduce_p.to_far()
        out_mine(mate, total)
        out_copy(0, 0, across).wait_recv()
        po_ref[2] = (total[...] + pi_ref[0].astype(F32)).astype(BF16)
        out_copy(2, 1, mate).start()
        reduce_o.finish()

    reduce_k.to_pair()
    reduce_k.to_near()

    @pl.when(inner)
    def _():
        reduce_p.keep_own()
        reduce_p.collect()
        og_ref[...] = kept_p[...].astype(BF16)
        ograd_copy().start()

    back.step(1)

    @pl.when(inner)
    def _():
        out_both(me, total)
        out_copy(1, 1, across).wait_recv()
        outputs_ref[...] = (
            x_ref[...].astype(F32) + total[...] + pi_ref[1].astype(F32)
        ).astype(BF16)
        reduce_o.keep_own()
        reduce_o.collect()

    reduce_q.to_far()
    reduce_q.keep_own()
    back.step(2)
    reduce_k.to_far()
    reduce_k.keep_own()

    @pl.when(edge)
    def _():
        out_mine(me, total)
        out_copy(2, 1, mate).wait_recv()
        outputs_ref[...] = (
            x_ref[...].astype(F32) + total[...] + pi_ref[1].astype(F32)
        ).astype(BF16)
        ograd_copy().wait_recv()
        ograd_ref[...] = og_ref[...].astype(F32)

    outputs_store = store(outputs_ref, outputs_hbm, 4)
    ograd_store = store(ograd_ref, ograd_hbm, 5)
    reduce_q.collect()
    reduce_k.collect()
    qgrad_store = store(qgrad_ref, qgrad_hbm, 6)
    back.finish()
    piece = x_ref[...].astype(F32)
    scale = row_scale(piece)
    weighted = total[...] * in_gain_ref[...]
    mean = jnp.mean(weighted * piece, axis=-1, keepdims=True)
    igrad_ref[...] = (
        held_c[row_at(me), :].astype(F32) + scale * weighted - scale * scale * scale * piece * mean
    ).astype(BF16)
    igrad_store = store(igrad_ref, igrad_hbm, 7)
    forward.finish()
    backward.finish()
    reduce_q.finish()
    reduce_k.finish()

    @pl.when(edge)
    def _():
        share.inward().wait_send()
        cot_copy(cot_hbm, me, 0, mate).wait_send()
        for origin in (across, beyond, mate, me):
            mixed_copy(origin).wait_send()

    @pl.when(inner)
    def _():
        share.finish()
        reduce_p.finish()
        cot_copy(cot_hbm, me, 0, across).wait_send()
        cot_copy(held_c.at[row_at(mate), :], mate, 1, across).wait_send()
        for origin in (me, across, beyond):
            grad_copy(origin).wait_send()
        out_copy(0, 0, across).wait_send()
        out_copy(1, 1, across).wait_send()
        out_copy(2, 1, mate).wait_send()
        ograd_copy().wait_send()
    for copy in (outputs_store, ograd_store, qgrad_store, igrad_store):
        copy.wait()


def hand_over(*refs):
    count = (len(refs) - 1) // 3
    sources, targets, held = refs[:count], refs[count : 2 * count], refs[2 * count : -1]
    sems = refs[-1]
    loads, stores = [], []
    for k in range(count):
        loads.append(pltpu.make_async_copy(sources[k], held[k], sems.at[0, k]))
        stores.append(pltpu.make_async_copy(held[k], targets[k], sems.at[1, k]))
        loads[k].start()
    for k in range(count):
        loads[k].wait()
        stores[k].start()
    for k in range(count):
        stores[k].wait()


def vmem(*shape, dtype=BF16):
    return pltpu.VMEM(shape, dtype)


def shards(inputs, norm_gain, qkv_weight, head_gain, out_weight, out_cotangent):
    rows, width = inputs.shape
    local_width = qkv_weight.shape[2]
    heads = local_width // DH
    n = lax.axis_size("tp")
    ctx_size = lax.axis_size("ctx")
    chips = ctx_size // 2
    block = rows * n
    slab = width // ctx_size
    factor = 1.0 / math.sqrt(block * ctx_size)
    dma = pltpu.SemaphoreType.DMA
    shape = jax.ShapeDtypeStruct
    m = math.isqrt(chips)
    state = [
        vmem(heads * DH, DH, dtype=F32),
        vmem(heads * DH, DH),
        vmem(heads * DH, DH),
        vmem(heads * DH // 2, DH),
        vmem(chips, heads * DH, DH),
        dma((2, chips + 1)),
        dma((2, chips)),
    ]

    def slabs(wide):
        return [
            vmem(2, m, m * slab, wide),
            vmem(2, m - 1, m * slab, wide),
            vmem(2, m - 1, slab, wide),
            dma((2, 2, m)),
            dma((2, 2, m)),
            dma((2, 2, m)),
        ]

    results = [
        shape((rows, width), BF16),
        shape((rows, width), BF16),
        shape((3, slab, local_width), F32),
        shape((slab, local_width), F32),
    ]
    staged = [vmem(*r.shape, dtype=r.dtype) for r in results]
    scratch = (
        staged
        + [vmem(3, width, local_width), vmem(3 * local_width, width)]
        + [vmem(2 * local_width, width), dma((8,))]
        + [vmem(m, m, 2, slab, block), vmem(block, 3 * local_width)]
        + [vmem(block, 2 * local_width), vmem(block, 3 * local_width)]
        + [vmem(rows, width), vmem(block, width), dma((2, n)), dma((n,))]
        + [vmem(block, width), vmem(m, m, 2, slab, block), dma((2,)), dma((n,))]
        + [vmem(block, local_width), dma((n,)), dma((n,)), dma((n,)), dma((n,))]
        + [dma((1 + 2 * chips,)), dma((ctx_size,))]
        + [vmem(rows, width, dtype=F32), vmem(3, rows, width), vmem(2, rows, width)]
        + [dma((3,)), dma((2,)), vmem(slab, local_width), dma((2,))]
        + [vmem(n, rows, width), vmem(n + 1, rows, width), dma((n,)), dma((n + 1,))]
        + [vmem(heads, block, block), vmem(block, local_width, dtype=F32)]
        + [vmem(block, local_width), vmem(block, local_width, dtype=F32)]
        + state
        + state
        + slabs(local_width // 2)
        + slabs(local_width)
        + [vmem(slab, local_width, dtype=F32)]
        + slabs(local_width // 2) * 2
    )
    held = pl.BlockSpec(memory_space=pltpu.VMEM)
    anywhere = pl.BlockSpec(memory_space=pl.ANY)
    made = pl.pallas_call(
        functools.partial(block_kernel, n, chips, factor),
        name="block",
        out_shape=results,
        in_specs=[anywhere] * 2 + [held] * 2 + [anywhere] * 2,
        out_specs=[anywhere] * 4,
        scratch_shapes=scratch,
        compiler_params=pltpu.CompilerParams(
            collective_id=0, has_side_effects=True, vmem_limit_bytes=VMEM_LIMIT
        ),
    )(
        inputs,
        out_cotangent,
        norm_gain.reshape(1, width),
        head_gain.reshape(1, local_width),
        qkv_weight.transpose(1, 0, 2),
        out_weight,
    )
    outputs, input_grad, qkv_grad, out_grad_t = pl.pallas_call(
        hand_over,
        name="hand_over",
        out_shape=results,
        in_specs=[anywhere] * 4,
        out_specs=[anywhere] * 4,
        scratch_shapes=staged + [dma((2, 4))],
    )(*made)
    return (outputs, input_grad, qkv_grad.transpose(1, 0, 2), out_grad_t)


def solution(mesh):
    in_specs = (
        P(("ctx", "tp"), None),
        P(),
        P(None, None, "tp"),
        P("tp"),
        P("tp", None),
        P(("ctx", "tp"), None),
    )
    out_specs = (
        P(("ctx", "tp"), None),
        P(("ctx", "tp"), None),
        P("ctx", None, "tp"),
        P("ctx", "tp"),
    )
    return jax.shard_map(shards, mesh=mesh, in_specs=in_specs, out_specs=out_specs, check_vma=False)
```

```python
import functools
import math

import jax
import jax.numpy as jnp
from jax import lax
from jax.experimental import pallas as pl
from jax.experimental.pallas import tpu as pltpu
from jax.sharding import PartitionSpec as P

DH = 128
EPSILON = 1e-05
MESH = pl.DeviceIdType.MESH
F32 = jnp.float32
BF16 = jnp.bfloat16
VMEM_LIMIT = 63 * 1024 * 1024
NN = (((1,), (0,)), ((), ()))
NT = (((1,), (1,)), ((), ()))
TN = (((0,), (0,)), ((), ()))


def dot(a, b, dims=NN):
    return lax.dot_general(a, b, dims, preferred_element_type=F32)


def row_scale(rows):
    return lax.rsqrt(jnp.mean(rows * rows, axis=-1, keepdims=True) + EPSILON)


def split(value):
    high = value.astype(BF16)
    return high, (value - high.astype(F32)).astype(BF16)


def with_state(rows, state, dims=NN):
    return dot(
        jnp.concatenate([rows, rows], axis=1),
        jnp.concatenate(split(state), axis=dims[0][1][0]),
        dims,
    )


def line_barrier(ctx, me, n, others):
    barrier = pltpu.get_barrier_semaphore()

    @pl.when(me > 0)
    def _():
        pl.semaphore_signal(barrier, inc=1, device_id=(ctx, me - 1), device_id_type=MESH)

    @pl.when(me < n - 1)
    def _():
        pl.semaphore_signal(barrier, inc=1, device_id=(ctx, me + 1), device_id_type=MESH)

    for other in others:
        pl.semaphore_signal(barrier, inc=1, device_id=(other, me), device_id_type=MESH)
    inner = jnp.logical_and(me > 0, me < n - 1)

    @pl.when(inner)
    def _():
        pl.semaphore_wait(barrier, 2 + len(others))

    @pl.when(jnp.logical_not(inner))
    def _():
        pl.semaphore_wait(barrier, 1 + len(others))


class LineGather:
    def __init__(self, ctx, me, n, own, held, send, recv):
        self.ctx, self.me, self.n = ctx, me, n
        self.own, self.held, self.send, self.recv = own, held, send, recv

    def at(self, origin):
        rows = self.own.shape[0]
        return self.held.at[pl.ds(pl.multiple_of(origin * rows, rows), rows), :]

    def copy(self, source, origin, up):
        target = self.me + 1 if up else self.me - 1
        return pltpu.make_async_remote_copy(
            src_ref=source,
            dst_ref=self.at(origin),
            send_sem=self.send.at[1 if up else 0, origin],
            recv_sem=self.recv.at[origin],
            device_id=(self.ctx, target),
            device_id_type=MESH,
        )

    def start_up(self):
        @pl.when(self.me < self.n - 1)
        def _():
            self.copy(self.own, self.me, True).start()

    def start_down(self):
        @pl.when(self.me > 0)
        def _():
            self.copy(self.own, self.me, False).start()

    def step(self, d):
        below, above = self.me - d, self.me + d

        @pl.when(below >= 0)
        def _():
            self.copy(self.at(below), below, True).wait_recv()

            @pl.when(self.me < self.n - 1)
            def _():
                self.copy(self.at(below), below, True).start()

        @pl.when(above < self.n)
        def _():
            self.copy(self.at(above), above, False).wait_recv()

            @pl.when(self.me > 0)
            def _():
                self.copy(self.at(above), above, False).start()

    def finish(self):
        for origin in range(self.n):

            @pl.when(jnp.logical_and(origin <= self.me, self.me < self.n - 1))
            def _():
                self.copy(self.at(origin), origin, True).wait_send()

            @pl.when(jnp.logical_and(origin >= self.me, self.me > 0))
            def _():
                self.copy(self.at(origin), origin, False).wait_send()


class LineScatter:
    def __init__(self, ctx, me, n, partial, total, out, arrived, send, recv):
        self.ctx, self.me, self.n = ctx, me, n
        self.partial, self.total, self.out = partial, total, out
        self.arrived = arrived
        self.send, self.recv = send, recv

    def copy(self, t, up, slot):
        target = self.me + 1 if up else self.me - 1
        return pltpu.make_async_remote_copy(
            src_ref=self.out.at[t],
            dst_ref=self.arrived.at[slot],
            send_sem=self.send.at[t],
            recv_sem=self.recv.at[slot],
            device_id=(self.ctx, target),
            device_id_type=MESH,
        )

    def add(self, slot):
        self.copy(0, True, slot).wait_recv()
        self.total[...] += self.arrived[slot].astype(F32)

    def step(self, s):
        me, n = self.me, self.n

        @pl.when(s >= me)
        def _():
            t = n - 1 - s + me
            self.partial(t, self.total)

            @pl.when(me > 0)
            def _():
                self.add(t)

            self.out[t] = self.total[...].astype(BF16)
            self.copy(t, True, t).start()

        @pl.when(s >= n - 1 - me)
        def _():
            t = s - (n - 1 - me)
            self.partial(t, self.total)

            @pl.when(me < n - 1)
            def _():
                self.add(t)

            self.out[t] = self.total[...].astype(BF16)
            self.copy(t, False, n if s == n - 2 else t).start()

    def finish(self):
        me, n = self.me, self.n
        self.partial(me, self.total)

        @pl.when(me > 0)
        def _():
            self.add(me)

        @pl.when(me < n - 1)
        def _():
            self.add(n)

        for t in range(n):

            @pl.when(t != me)
            def _():
                self.copy(t, True, t).wait_send()


class StateSum:
    def __init__(self, ctx, me, chips, later, local, mine, pair, chip_sum, arrived, sems, turns):
        self.chip, self.core = ctx // 2, lax.rem(ctx, 2)
        self.sibling = ctx + 1 - 2 * self.core
        self.me, self.chips, self.later = me, chips, later
        self.local, self.mine, self.pair = local, mine, pair
        self.chip_sum, self.arrived = chip_sum, arrived
        self.sems, self.turns = sems, turns
        half = chip_sum.shape[0]
        self.half = pl.ds(pl.multiple_of(self.core * half, half), half)

    def pair_copy(self):
        return pltpu.make_async_remote_copy(
            src_ref=self.mine,
            dst_ref=self.pair,
            send_sem=self.sems.at[0, 0],
            recv_sem=self.sems.at[1, 0],
            device_id=(self.sibling, self.me),
            device_id_type=MESH,
        )

    def chip_copy(self, target, origin):
        return pltpu.make_async_remote_copy(
            src_ref=self.chip_sum,
            dst_ref=self.arrived.at[origin, self.half, :],
            send_sem=self.sems.at[0, target + 1],
            recv_sem=self.sems.at[1, origin + 1],
            device_id=(2 * target + self.core, self.me),
            device_id_type=MESH,
        )

    def core_copy(self, origin):
        piece = self.arrived.at[origin, self.half, :]
        return pltpu.make_async_remote_copy(
            src_ref=piece,
            dst_ref=piece,
            send_sem=self.turns.at[0, origin],
            recv_sem=self.turns.at[1, origin],
            device_id=(self.sibling, self.me),
            device_id_type=MESH,
        )

    def wanted(self, source, target):
        return source > target if self.later else source < target

    def start(self):
        self.mine[...] = self.local[...].astype(BF16)
        self.pair_copy().start()

    def spread(self):
        self.pair_copy().wait()
        own = self.local[self.half, :] + self.pair[self.half, :].astype(F32)
        self.chip_sum[...] = own.astype(BF16)
        for other in range(self.chips):

            @pl.when(self.wanted(self.chip, other))
            def _():
                self.chip_copy(other, self.chip).start()

    def hand_on(self):
        for other in range(self.chips):

            @pl.when(self.wanted(other, self.chip))
            def _():
                self.chip_copy(other, other).wait_recv()
                self.core_copy(other).start()

    def collect(self):
        near = self.core == (0 if self.later else 1)
        self.local[...] = jnp.where(near, self.pair[...].astype(F32), 0.0)
        for other in range(self.chips):

            @pl.when(self.wanted(other, self.chip))
            def _():
                self.core_copy(other).wait_recv()
                self.local[...] += self.arrived[other].astype(F32)

    def finish(self):
        for other in range(self.chips):

            @pl.when(self.wanted(other, self.chip))
            def _():
                self.core_copy(other).wait_send()

            @pl.when(self.wanted(self.chip, other))
            def _():
                self.chip_copy(other, self.chip).wait_send()


class SlabReduce:
    def __init__(self, ctx, me, chips, factor, left, parts, kept, stores, arrivals, sems):
        self.chip, self.core = ctx // 2, lax.rem(ctx, 2)
        self.sibling = ctx + 1 - 2 * self.core
        self.me, self.chips, self.factor = me, chips, factor
        self.left, self.parts, self.kept, self.stores = left, parts, kept, stores
        self.pair_in, self.near_in, self.far_in = arrivals
        self.pair_sems, self.near_sems, self.far_sems = sems
        self.m = self.near_in.shape[1] + 1
        self.slab, self.wide = self.far_in.shape[2:]
        low, high = lax.rem(self.chip, self.m), self.chip // self.m
        self.first, self.second = (low, high), (high, low)

    def chip_of(self, side, first, second):
        return second * self.m + first if side == 0 else first * self.m + second

    def held(self, side, start, size):
        ref, column = self.stores[side]
        depth = ref.shape[0]
        row = pl.multiple_of(lax.rem(start, depth), size)
        column = pl.multiple_of(start // depth * 2 * self.wide + column, self.wide)
        return ref.at[pl.ds(row, size), pl.ds(column, self.wide)]

    def near_out(self, side, j):
        size = self.m * self.slab
        return self.held(side, self.chips * self.slab + (j - 1) * size, size)

    def far_out(self, side, j):
        start = (self.chips + self.m * (self.m - 1) + j - 1) * self.slab
        return self.held(side, start, self.slab)

    def times(self, rows, side):
        right, base = self.parts[side]
        return dot(rows, right[:, base : base + self.wide]) * self.factor

    def one_slab(self, side, second):
        first = self.first[side]
        high, low = (second, first) if side == 0 else (first, second)
        value = self.times(self.left[high, low, self.core], side)
        at = pl.ds(pl.multiple_of(low * self.slab, self.slab), self.slab)
        value = value + self.pair_in[side, high, at, :].astype(F32)
        row = pl.multiple_of(second * self.slab, self.slab)
        for j in range(1, self.m):
            value = value + self.near_in[side, j - 1, pl.ds(row, self.slab), :].astype(F32)
        return value

    def pair_copy(self, side, k):
        size = self.m * self.slab
        return pltpu.make_async_remote_copy(
            src_ref=self.held(side, k * size, size),
            dst_ref=self.pair_in.at[side, k],
            send_sem=self.pair_sems.at[0, side, k],
            recv_sem=self.pair_sems.at[1, side, k],
            device_id=(self.sibling, self.me), device_id_type=MESH,
        )

    def near_copy(self, side, j):
        first = lax.rem(self.first[side] + j, self.m)
        target = self.chip_of(side, first, self.second[side])
        return pltpu.make_async_remote_copy(
            src_ref=self.near_out(side, j), dst_ref=self.near_in.at[side, j - 1],
            send_sem=self.near_sems.at[0, side, j], recv_sem=self.near_sems.at[1, side, j],
            device_id=(2 * target + self.core, self.me), device_id_type=MESH,
        )

    def far_copy(self, side, j):
        second = lax.rem(self.second[side] + j, self.m)
        target = self.chip_of(side, self.first[side], second)
        return pltpu.make_async_remote_copy(
            src_ref=self.far_out(side, j), dst_ref=self.far_in.at[side, j - 1],
            send_sem=self.far_sems.at[0, side, j], recv_sem=self.far_sems.at[1, side, j],
            device_id=(2 * target + self.core, self.me), device_id_type=MESH,
        )

    def to_pair(self):
        size = self.m * self.slab

        @pl.loop(0, self.m)
        def _(k):
            rows = self.left[k, :, 1 - self.core]
            rows = rows.reshape(size, rows.shape[-1])
            for side in range(2):
                self.held(side, k * size, size)[...] = self.times(rows, side).astype(BF16)
                self.pair_copy(side, k).start()

    def to_near(self):
        for side in range(2):
            @pl.loop(0, self.m)
            def _(k):
                self.pair_copy(side, k).wait_recv()

            @pl.loop(1, self.m)
            def _(j):
                first = lax.rem(self.first[side] + j, self.m)
                first_rows = pl.ds(pl.multiple_of(first * self.slab, self.slab), self.slab)
                if side == 0:
                    rows, pair = self.left[:, first, self.core], self.pair_in[side, :, first_rows]
                else:
                    rows, pair = self.left[first, :, self.core], self.pair_in[side, first]
                size = self.m * self.slab
                value = self.times(rows.reshape(size, rows.shape[-1]), side)
                value = value + pair.reshape(size, self.wide).astype(F32)
                self.near_out(side, j)[...] = value.astype(BF16)
                self.near_copy(side, j).start()

    def to_far(self):
        for side in range(2):

            @pl.loop(1, self.m)
            def _(j):
                self.near_copy(side, j).wait_recv()

            @pl.loop(1, self.m)
            def _(j):
                second = lax.rem(self.second[side] + j, self.m)
                self.far_out(side, j)[...] = self.one_slab(side, second).astype(BF16)
                self.far_copy(side, j).start()

    def keep_own(self):
        for side in range(2):
            ref, column = self.kept[side]
            ref[:, column : column + self.wide] = self.one_slab(side, self.second[side])

    def collect(self):
        for side in range(2):
            ref, column = self.kept[side]

            @pl.loop(1, self.m)
            def _(j):
                self.far_copy(side, j).wait_recv()
                ref[:, column : column + self.wide] += self.far_in[side, j - 1].astype(F32)

    def finish(self):
        for side in range(2):

            @pl.loop(0, self.m)
            def _(k):
                self.pair_copy(side, k).wait_send()

            @pl.loop(1, self.m)
            def _(j):
                self.near_copy(side, j).wait_send()
                self.far_copy(side, j).wait_send()


class Share:
    def __init__(self, ctx, me, partner, chips, source, held, send, recv):
        self.ctx, self.me, self.partner, self.chips = ctx, me, partner, chips
        self.chip, self.core = ctx // 2, lax.rem(ctx, 2)
        self.source, self.held, self.send, self.recv = source, held, send, recv

    def at(self, ref, origin):
        rows = self.held.shape[0] // (2 * self.chips)
        return ref.at[pl.ds(pl.multiple_of(origin * rows, rows), rows), :]

    def copy(self, source, origin, sem, target):
        return pltpu.make_async_remote_copy(
            src_ref=self.at(source, origin), dst_ref=self.at(self.held, origin),
            send_sem=self.send.at[sem], recv_sem=self.recv.at[origin],
            device_id=target, device_id_type=MESH,
        )

    def inward(self):
        return self.copy(self.source, self.ctx, 0, (self.ctx, self.partner))

    def to_chip(self, p):
        return self.copy(self.held, self.ctx, 1 + p, (2 * p + self.core, self.me))

    def to_sibling(self, p):
        target = (self.ctx + 1 - 2 * self.core, self.me)
        return self.copy(self.held, 2 * p + self.core, 1 + self.chips + p, target)

    def arrival(self, origin):
        self.copy(self.held, origin, 0, (self.ctx, self.partner)).wait_recv()

    def spread(self):
        self.arrival(self.ctx)

        @pl.loop(1, self.chips)
        def _(j):
            self.to_chip(lax.rem(self.chip + j, self.chips)).start()

        self.to_sibling(self.chip).start()

    def hand_on(self):
        @pl.loop(1, self.chips)
        def _(j):
            p = lax.rem(self.chip + self.chips - j, self.chips)
            self.arrival(2 * p + self.core)
            self.to_sibling(p).start()

    def complete(self):
        @pl.loop(0, self.chips)
        def _(p):
            self.arrival(2 * p + 1 - self.core)

    def finish(self):
        @pl.loop(0, self.chips)
        def _(p):
            self.to_sibling(p).wait_send()

        @pl.loop(1, self.chips)
        def _(j):
            self.to_chip(lax.rem(self.chip + j, self.chips)).wait_send()


def block_kernel(
    n, chips, factor,
    x_hbm, cot_hbm, in_gain_ref, gain_ref, w_hbm, wo_hbm,
    outputs_hbm, igrad_hbm, qgrad_hbm, ograd_hbm,
    outputs_ref, igrad_ref, qgrad_ref, ograd_ref,
    w_ref, wt_ref, both_wo, load,
    normt_ref, proj_ref, both_mixed, gproj_ref,
    x_ref, held_x, xsend, xrecv,
    held_c, cott_ref, csend, crecv,
    gm_ref, gsend, grecv, msend, mrecv, wsend, wrecv,
    total, po_ref, pi_ref, osend, orecv, og_ref, ogsem,
    back_out, back_in, bsend, brecv,
    scores, attended, gatt, gkey, gval,
    local_f, mine_f, pair_f, sum_f, arrived_f, sems_f, turns_f,
    local_b, mine_b, pair_b, sum_b, arrived_b, sems_b, turns_b,
    q0, q1, q2, q3, q4, q5, k0, k1, k2, k3, k4, k5,
    kept_p, o0, o1, o2, o3, o4, o5, p0, p1, p2, p3, p4, p5,
):
    ctx, me = lax.axis_index("ctx"), lax.axis_index("tp")
    rows = x_hbm.shape[0]
    block, width = both_mixed.shape[0], both_mixed.shape[1] // 2
    mixed_ref, mixp_ref = both_mixed.at[:, :width], both_mixed.at[:, width:]
    wo_ref, wop_ref = both_wo.at[:width], both_wo.at[width:]
    heads = width // DH
    chip, core = ctx // 2, lax.rem(ctx, 2)
    mate = me + 1 - 2 * lax.rem(me, 2)
    across = n - 1 - me
    beyond = n - 1 - mate
    edge = jnp.logical_or(me == 0, me == n - 1)
    inner = jnp.logical_not(edge)

    def store(source, target, sem):
        copy = pltpu.make_async_copy(source, target, load.at[sem])
        copy.start()
        return copy

    def row_at(origin):
        return pl.ds(pl.multiple_of(origin * rows, rows), rows)

    def cols(h, part=0):
        if isinstance(h, int):
            return slice(part * width + h * DH, part * width + (h + 1) * DH)
        return pl.ds(pl.multiple_of(part * width + h * DH, DH), DH)

    def head_rows(h):
        if isinstance(h, int):
            return slice(h * DH, (h + 1) * DH)
        return pl.ds(pl.multiple_of(h * DH, DH), DH)

    def each_head(body):
        for h in range(heads):
            body(h)

    def causal(value):
        down = lax.broadcasted_iota(jnp.int32, (block, block), 0)
        along = lax.broadcasted_iota(jnp.int32, (block, block), 1)
        return jnp.where(down >= along, value, 0.0).astype(BF16)

    x_load = pltpu.make_async_copy(x_hbm, x_ref, load.at[0])
    w_load = pltpu.make_async_copy(w_hbm, w_ref, load.at[1])
    c_load = pltpu.make_async_copy(cot_hbm, held_c.at[row_at(me), :], load.at[2])
    wo_load = pltpu.make_async_copy(wo_hbm, wo_ref, load.at[3])
    x_load.start()
    w_load.start()
    c_load.start()
    wo_load.start()
    others = [ctx + 1 - 2 * core]
    others += [2 * lax.rem(chip + j, chips) + core for j in range(1, chips)]
    line_barrier(ctx, me, n, others)
    gather_x = LineGather(ctx, me, n, x_hbm, held_x, xsend, xrecv)
    share = Share(ctx, me, mate, chips, wo_hbm, wop_ref, wsend, wrecv)
    forward = StateSum(
        ctx, me, chips, False, local_f, mine_f, pair_f, sum_f, arrived_f, sems_f, turns_f
    )
    backward = StateSum(
        ctx, me, chips, True, local_b, mine_b, pair_b, sum_b, arrived_b, sems_b, turns_b
    )
    half = width // 2
    reduce_q = SlabReduce(
        ctx, me, chips, factor, normt_ref, [(gproj_ref, 0), (gproj_ref, half)],
        [(qgrad_ref.at[0], 0), (qgrad_ref.at[0], half)],
        [(w_ref.at[0], 0), (w_ref.at[0], half)], (q0, q1, q2), (q3, q4, q5),
    )
    reduce_k = SlabReduce(
        ctx, me, chips, factor, normt_ref, [(gproj_ref, width), (gproj_ref, 2 * width)],
        [(qgrad_ref.at[1], 0), (qgrad_ref.at[2], 0)],
        [(w_ref.at[1], 0), (w_ref.at[2], 0)], (k0, k1, k2), (k3, k4, k5),
    )
    reduce_o = SlabReduce(
        ctx, me, chips, factor, cott_ref, [(mixed_ref, 0), (mixed_ref, half)],
        [(ograd_ref, 0), (ograd_ref, half)],
        [(w_ref.at[1], 0), (w_ref.at[1], half)], (o0, o1, o2), (o3, o4, o5),
    )
    reduce_p = SlabReduce(
        ctx, me, chips, factor, cott_ref, [(mixp_ref, 0), (mixp_ref, half)],
        [(kept_p, 0), (kept_p, half)],
        [(held_x, 0), (held_x, half)], (p0, p1, p2), (p3, p4, p5),
    )

    def remote(source, target, send, recv, device):
        return pltpu.make_async_remote_copy(
            src_ref=source, dst_ref=target, send_sem=send, recv_sem=recv,
            device_id=(ctx, device), device_id_type=MESH,
        )

    def cot_copy(source, origin, sem, device):
        return remote(
            source, held_c.at[row_at(origin), :], csend.at[sem], crecv.at[origin], device
        )

    def grad_copy(origin):
        piece = gm_ref.at[row_at(origin), :]
        return remote(piece, piece, gsend.at[origin], grecv.at[origin], mate)

    def mixed_copy(origin):
        at = row_at(origin)
        return remote(
            mixed_ref.at[at, :], mixp_ref.at[at, :], msend.at[origin], mrecv.at[origin], mate
        )

    def out_copy(slot, landing, device):
        return remote(
            po_ref.at[slot], pi_ref.at[landing], osend.at[slot], orecv.at[landing], device
        )

    def ograd_copy():
        return remote(og_ref, og_ref, ogsem.at[0], ogsem.at[1], mate)

    def project(source, origin):
        at = row_at(origin)
        piece = source[...].astype(F32)
        normed = (piece * row_scale(piece) * in_gain_ref[...]).astype(BF16)
        for part in range(3):
            here = slice(part * width, (part + 1) * width)
            proj_ref[at, here] = dot(normed, w_ref[part]).astype(BF16)
        normt_ref[:, :, :, :, at] = normed.T.reshape(normt_ref.shape[:4] + (rows,))

    def turn_weight(first, last):
        step = 2 * DH
        count = w_ref.shape[1] // step

        @pl.loop(first, last)
        def _(k):
            part = k // count
            at = pl.ds(pl.multiple_of(lax.rem(k, count) * step, step), step)
            into = pl.ds(pl.multiple_of(part * width, width), width)
            wt_ref[into, at] = w_ref[part, at, :].T

    gather_x.start_up()
    gather_x.start_down()
    x_load.wait()
    w_load.wait()
    project(x_ref, me)
    turns = 3 * w_ref.shape[1] // (2 * DH)
    turn_weight(0, turns // 2)

    @pl.loop(1, n)
    def _(d):
        @pl.when(jnp.logical_and(inner, d == 2))
        def _():
            share.spread()

        gather_x.step(d)

        @pl.when(jnp.logical_and(edge, d == 1))
        def _():
            share.inward().start()

        @pl.when(jnp.logical_and(inner, d == 2))
        def _():
            cot_copy(cot_hbm, me, 0, across).start()

        @pl.when(me - d >= 0)
        def _():
            project(gather_x.at(me - d), me - d)

        @pl.when(me + d < n)
        def _():
            project(gather_x.at(me + d), me + d)

        @pl.when(d == 1)
        def _():
            turn_weight(turns // 2, turns)

            @pl.when(edge)
            def _():
                share.inward().wait_send()
                cot_copy(cot_hbm, me, 0, mate).start()

    @each_head
    def _(h):
        local_f[head_rows(h), :] = dot(proj_ref[:, cols(h, 1)], proj_ref[:, cols(h, 2)], TN)

    forward.start()

    @each_head
    def _(h):
        scores[h] = causal(dot(proj_ref[:, cols(h)], proj_ref[:, cols(h, 1)], NT))

    forward.spread()

    @each_head
    def _(h):
        attended[:, cols(h)] = dot(scores[h], proj_ref[:, cols(h, 2)])

    wo_load.wait()
    c_load.wait()

    @pl.when(edge)
    def _():
        total[:, :width] = dot(held_c[row_at(me), :], wo_ref[...], NT)

    forward.hand_on()

    @pl.when(inner)
    def _():
        share.hand_on()
        cot_copy(cot_hbm, mate, 0, mate).wait_recv()
        cot_copy(held_c.at[row_at(mate), :], mate, 1, across).start()

    forward.collect()

    @each_head
    def _(h):
        query = proj_ref[:, cols(h)]
        value = attended[:, cols(h)] + with_state(query, local_f[head_rows(h), :])
        attended[:, cols(h)] = value
        mixed_ref[:, cols(h)] = (value * row_scale(value) * gain_ref[:, cols(h)]).astype(BF16)


    def grad_rows(at, value):
        weighted = value * gain_ref[...]
        for h in range(heads):
            here = slice(h * DH, (h + 1) * DH)
            value = attended[at, here]
            scale = row_scale(value)
            part = weighted[:, here]
            mean = jnp.mean(part * value, axis=-1, keepdims=True)
            gatt[at, here] = (scale * part - scale * scale * scale * value * mean).astype(BF16)

    def rows_from(origin, count=1):
        return pl.ds(pl.multiple_of(origin * rows, rows), count * rows)

    def own_rows(origin, count=1):
        at = rows_from(origin, count)
        grad_rows(at, dot(held_c[at, :], wo_ref[...], NT))

    def mate_rows(origin, count=1):
        at = rows_from(origin, count)
        gm_ref[at, :] = dot(held_c[at, :], wop_ref[...], NT).astype(BF16)
        for k in range(count):
            grad_copy(origin + k).start()

    def turn_cot(origin):
        at = row_at(origin)
        cott_ref[:, :, :, :, at] = held_c[at, :].T.reshape(cott_ref.shape[:4] + (rows,))

    low = me // 2
    last = (n - 1) * (1 - low)

    def attend_back(h, at, first, count):
        query, grad = proj_ref[at, cols(h)], gatt[at, cols(h)]
        key, value = proj_ref[:, cols(h, 1)], proj_ref[:, cols(h, 2)]
        down = lax.broadcasted_iota(jnp.int32, (count, block), 0) + first
        along = lax.broadcasted_iota(jnp.int32, (count, block), 1)
        raw = dot(grad, value, NT)
        gscores = jnp.where(down >= along, raw, 0.0).astype(BF16)
        gquery = dot(gscores, key) + with_state(grad, local_f[head_rows(h), :], NT)
        gproj_ref[at, cols(h)] = gquery.astype(BF16)
        return dot(gscores, query, TN), dot(scores[h, at, :], grad, TN)

    @pl.when(edge)
    def _():
        for origin in (across, beyond, mate, me):
            mixed_copy(origin).start()
        grad_rows(row_at(me), total[:, :width])
        for origin in (mate, beyond):
            grad_copy(origin).wait_recv()
        here = rows_from(1, n - 2)
        grad_rows(here, gm_ref[here, :].astype(F32))

    @pl.when(inner)
    def _():
        share.complete()
        cot_copy(cot_hbm, across, 0, across).wait_recv()
        mate_rows(1, n - 2)
        own_rows(me - 1, n - 1)

    most = rows_from(low, n - 1)

    @each_head
    def _(h):
        local_b[head_rows(h), :] = dot(proj_ref[most, cols(h)], gatt[most, cols(h)], TN)
        gk, gv = attend_back(h, most, low * rows, (n - 1) * rows)
        gkey[:, cols(h)] = gk
        gval[:, cols(h)] = gv

    @pl.when(edge)
    def _():
        grad_copy(across).wait_recv()
        grad_rows(row_at(across), gm_ref[row_at(across), :].astype(F32))

    @pl.when(inner)
    def _():
        turn_cot(me)
        turn_cot(mate)
        turn_cot(across)
        cot_copy(cot_hbm, beyond, 0, across).wait_recv()
        mate_rows(beyond)
        own_rows(beyond)

    @each_head
    def _(h):
        at = row_at(last)
        local_b[head_rows(h), :] += dot(proj_ref[at, cols(h)], gatt[at, cols(h)], TN)

    backward.start()

    @pl.when(inner)
    def _():
        turn_cot(beyond)
        reduce_o.to_pair()

    backward.spread()

    @each_head
    def _(h):
        gk, gv = attend_back(h, row_at(last), last * rows, rows)
        gkey[:, cols(h)] += gk
        gval[:, cols(h)] += gv

    @pl.when(inner)
    def _():
        reduce_o.to_near()

    def out_mine(origin, into):
        into[...] = dot(mixed_ref[row_at(origin), :], wo_ref[...])

    def out_both(origin, into):
        into[...] = dot(both_mixed[row_at(origin), :], both_wo[...])

    backward.hand_on()
    gather_x.finish()

    @pl.when(inner)
    def _():
        for slot, origin in enumerate((beyond, across)):
            mixed_copy(origin).wait_recv()
            out_both(origin, total)
            po_ref[slot] = total[...].astype(BF16)
            out_copy(slot, slot, across).start()
        mixed_copy(mate).wait_recv()
        mixed_copy(me).wait_recv()
        reduce_p.to_pair()
        reduce_o.to_far()
        reduce_p.to_near()

    backward.collect()

    @each_head
    def _(h):
        state = local_b[head_rows(h), :]
        key, value = proj_ref[:, cols(h, 1)], proj_ref[:, cols(h, 2)]
        gk = gkey[:, cols(h)] + with_state(value, state, NT)
        gv = gval[:, cols(h)] + with_state(key, state)
        gproj_ref[:, cols(h, 1)] = gk.astype(BF16)
        gproj_ref[:, cols(h, 2)] = gv.astype(BF16)

    def in_partial(t, into):
        into[...] = dot(gproj_ref[row_at(t), :], wt_ref[...])

    back = LineScatter(ctx, me, n, in_partial, total, back_out, back_in, bsend, brecv)
    back.step(0)
    reduce_q.to_pair()
    reduce_q.to_near()

    @pl.when(inner)
    def _():
        reduce_p.to_far()
        out_mine(mate, total)
        out_copy(0, 0, across).wait_recv()
        po_ref[2] = (total[...] + pi_ref[0].astype(F32)).astype(BF16)
        out_copy(2, 1, mate).start()
        reduce_o.finish()

    reduce_k.to_pair()
    reduce_k.to_near()

    back.step(1)

    @pl.when(inner)
    def _():
        reduce_p.keep_own()
        reduce_p.collect()
        og_ref[...] = kept_p[...].astype(BF16)
        ograd_copy().start()
        out_both(me, total)
        out_copy(1, 1, across).wait_recv()
        outputs_ref[...] = (
            x_ref[...].astype(F32) + total[...] + pi_ref[1].astype(F32)
        ).astype(BF16)
        reduce_o.keep_own()
        reduce_o.collect()

    reduce_q.to_far()
    reduce_q.keep_own()
    back.step(2)
    reduce_k.to_far()
    reduce_k.keep_own()

    @pl.when(edge)
    def _():
        out_mine(me, total)
        out_copy(2, 1, mate).wait_recv()
        outputs_ref[...] = (
            x_ref[...].astype(F32) + total[...] + pi_ref[1].astype(F32)
        ).astype(BF16)
        ograd_copy().wait_recv()
        ograd_ref[...] = og_ref[...].astype(F32)

    outputs_store = store(outputs_ref, outputs_hbm, 4)
    ograd_store = store(ograd_ref, ograd_hbm, 5)
    reduce_q.collect()
    reduce_k.collect()
    qgrad_store = store(qgrad_ref, qgrad_hbm, 6)
    back.finish()
    piece = x_ref[...].astype(F32)
    scale = row_scale(piece)
    weighted = total[...] * in_gain_ref[...]
    mean = jnp.mean(weighted * piece, axis=-1, keepdims=True)
    igrad_ref[...] = (
        held_c[row_at(me), :].astype(F32) + scale * weighted - scale * scale * scale * piece * mean
    ).astype(BF16)
    igrad_store = store(igrad_ref, igrad_hbm, 7)
    forward.finish()
    backward.finish()
    reduce_q.finish()
    reduce_k.finish()

    @pl.when(edge)
    def _():
        cot_copy(cot_hbm, me, 0, mate).wait_send()
        for origin in (across, beyond, mate, me):
            mixed_copy(origin).wait_send()

    @pl.when(inner)
    def _():
        share.finish()
        reduce_p.finish()
        cot_copy(cot_hbm, me, 0, across).wait_send()
        cot_copy(held_c.at[row_at(mate), :], mate, 1, across).wait_send()
        for origin in (me, across, beyond):
            grad_copy(origin).wait_send()
        out_copy(0, 0, across).wait_send()
        out_copy(1, 1, across).wait_send()
        out_copy(2, 1, mate).wait_send()
        ograd_copy().wait_send()
    for copy in (outputs_store, ograd_store, qgrad_store, igrad_store):
        copy.wait()


def hand_over(*refs):
    count = (len(refs) - 1) // 3
    sources, targets, held = refs[:count], refs[count : 2 * count], refs[2 * count : -1]
    sems = refs[-1]
    loads, stores = [], []
    for k in range(count):
        parts = sems.shape[2]
        for part in range(parts):
            axis = len(held[k].shape) - 2
            size = held[k].shape[axis] // parts
            at = (slice(None),) * axis + (pl.ds(part * size, size),)
            loads.append(pltpu.make_async_copy(sources[k].at[at], held[k].at[at], sems.at[0, k, part]))
            stores.append(pltpu.make_async_copy(held[k].at[at], targets[k].at[at], sems.at[1, k, part]))
    for copy in loads:
        copy.start()
    for k, copy in enumerate(loads):
        copy.wait()
        stores[k].start()
    for copy in stores:
        copy.wait()


def vmem(*shape, dtype=BF16):
    return pltpu.VMEM(shape, dtype)


def shards(inputs, norm_gain, qkv_weight, head_gain, out_weight, out_cotangent):
    rows, width = inputs.shape
    local_width = qkv_weight.shape[2]
    heads = local_width // DH
    n = lax.axis_size("tp")
    ctx_size = lax.axis_size("ctx")
    chips = ctx_size // 2
    block = rows * n
    slab = width // ctx_size
    factor = 1.0 / math.sqrt(block * ctx_size)
    dma = pltpu.SemaphoreType.DMA
    shape = jax.ShapeDtypeStruct
    m = math.isqrt(chips)
    state = [
        vmem(heads * DH, DH, dtype=F32),
        vmem(heads * DH, DH),
        vmem(heads * DH, DH),
        vmem(heads * DH // 2, DH),
        vmem(chips, heads * DH, DH),
        dma((2, chips + 1)),
        dma((2, chips)),
    ]

    def slabs(wide):
        return [
            vmem(2, m, m * slab, wide),
            vmem(2, m - 1, m * slab, wide),
            vmem(2, m - 1, slab, wide),
            dma((2, 2, m)),
            dma((2, 2, m)),
            dma((2, 2, m)),
        ]

    results = [
        shape((rows, width), BF16),
        shape((rows, width), BF16),
        shape((3, slab, local_width), F32),
        shape((slab, local_width), F32),
    ]
    staged = [vmem(*r.shape, dtype=r.dtype) for r in results]
    scratch = (
        staged
        + [vmem(3, width, local_width), vmem(3 * local_width, width)]
        + [vmem(2 * local_width, width), dma((8,))]
        + [vmem(m, m, 2, slab, block), vmem(block, 3 * local_width)]
        + [vmem(block, 2 * local_width), vmem(block, 3 * local_width)]
        + [vmem(rows, width), vmem(block, width), dma((2, n)), dma((n,))]
        + [vmem(block, width), vmem(m, m, 2, slab, block), dma((2,)), dma((n,))]
        + [vmem(block, local_width), dma((n,)), dma((n,)), dma((n,)), dma((n,))]
        + [dma((1 + 2 * chips,)), dma((ctx_size,))]
        + [vmem(rows, width, dtype=F32), vmem(3, rows, width), vmem(2, rows, width)]
        + [dma((3,)), dma((2,)), vmem(slab, local_width), dma((2,))]
        + [vmem(n, rows, width), vmem(n + 1, rows, width), dma((n,)), dma((n + 1,))]
        + [vmem(heads, block, block), vmem(block, local_width, dtype=F32)]
        + [vmem(block, local_width)]
        + [vmem(block, local_width, dtype=F32)] * 2
        + state
        + state
        + slabs(local_width // 2)
        + slabs(local_width)
        + [vmem(slab, local_width, dtype=F32)]
        + slabs(local_width // 2) * 2
    )
    held = pl.BlockSpec(memory_space=pltpu.VMEM)
    anywhere = pl.BlockSpec(memory_space=pl.ANY)
    made = pl.pallas_call(
        functools.partial(block_kernel, n, chips, factor),
        name="block",
        out_shape=results,
        in_specs=[anywhere] * 2 + [held] * 2 + [anywhere] * 2,
        out_specs=[anywhere] * 4,
        scratch_shapes=scratch,
        compiler_params=pltpu.CompilerParams(
            collective_id=0, has_side_effects=True, vmem_limit_bytes=VMEM_LIMIT
        ),
    )(
        inputs,
        out_cotangent,
        norm_gain.reshape(1, width),
        head_gain.reshape(1, local_width),
        qkv_weight.transpose(1, 0, 2),
        out_weight,
    )
    outputs, input_grad, qkv_grad, out_grad_t = pl.pallas_call(
        hand_over,
        name="hand_over",
        out_shape=results,
        in_specs=[anywhere] * 4,
        out_specs=[anywhere] * 4,
        scratch_shapes=staged + [dma((2, 4, 2))],
    )(*made)
    return (outputs, input_grad, qkv_grad.transpose(1, 0, 2), out_grad_t)


def solution(mesh):
    in_specs = (
        P(("ctx", "tp"), None),
        P(),
        P(None, None, "tp"),
        P("tp"),
        P("tp", None),
        P(("ctx", "tp"), None),
    )
    out_specs = (
        P(("ctx", "tp"), None),
        P(("ctx", "tp"), None),
        P("ctx", None, "tp"),
        P("ctx", "tp"),
    )
    return jax.shard_map(shards, mesh=mesh, in_specs=in_specs, out_specs=out_specs, check_vma=False)
```

```python
import functools
import math

import jax
import jax.numpy as jnp
from jax import lax
from jax.experimental import pallas as pl
from jax.experimental.pallas import tpu as pltpu
from jax.sharding import PartitionSpec as P

DH = 128
EPSILON = 1e-05
MESH = pl.DeviceIdType.MESH
F32 = jnp.float32
BF16 = jnp.bfloat16
VMEM_LIMIT = 63 * 1024 * 1024
NN = (((1,), (0,)), ((), ()))
NT = (((1,), (1,)), ((), ()))
TN = (((0,), (0,)), ((), ()))


def dot(a, b, dims=NN):
    return lax.dot_general(a, b, dims, preferred_element_type=F32)


def row_scale(rows):
    return lax.rsqrt(jnp.mean(rows * rows, axis=-1, keepdims=True) + EPSILON)


def split(value):
    high = value.astype(BF16)
    return high, (value - high.astype(F32)).astype(BF16)


def with_state(rows, state, dims=NN):
    return dot(
        jnp.concatenate([rows, rows], axis=1),
        jnp.concatenate(split(state), axis=dims[0][1][0]),
        dims,
    )


def line_barrier(ctx, me, n, others):
    barrier = pltpu.get_barrier_semaphore()

    @pl.when(me > 0)
    def _():
        pl.semaphore_signal(barrier, inc=1, device_id=(ctx, me - 1), device_id_type=MESH)

    @pl.when(me < n - 1)
    def _():
        pl.semaphore_signal(barrier, inc=1, device_id=(ctx, me + 1), device_id_type=MESH)

    for other in others:
        pl.semaphore_signal(barrier, inc=1, device_id=(other, me), device_id_type=MESH)
    inner = jnp.logical_and(me > 0, me < n - 1)

    @pl.when(inner)
    def _():
        pl.semaphore_wait(barrier, 2 + len(others))

    @pl.when(jnp.logical_not(inner))
    def _():
        pl.semaphore_wait(barrier, 1 + len(others))


class LineGather:
    def __init__(self, ctx, me, n, own, held, send, recv):
        self.ctx, self.me, self.n = ctx, me, n
        self.own, self.held, self.send, self.recv = own, held, send, recv

    def at(self, origin):
        rows = self.own.shape[0]
        return self.held.at[pl.ds(pl.multiple_of(origin * rows, rows), rows), :]

    def copy(self, source, origin, up):
        target = self.me + 1 if up else self.me - 1
        return pltpu.make_async_remote_copy(
            src_ref=source,
            dst_ref=self.at(origin),
            send_sem=self.send.at[1 if up else 0, origin],
            recv_sem=self.recv.at[origin],
            device_id=(self.ctx, target),
            device_id_type=MESH,
        )

    def start_up(self):
        @pl.when(self.me < self.n - 1)
        def _():
            self.copy(self.own, self.me, True).start()

    def start_down(self):
        @pl.when(self.me > 0)
        def _():
            self.copy(self.own, self.me, False).start()

    def step(self, d):
        below, above = self.me - d, self.me + d

        @pl.when(below >= 0)
        def _():
            self.copy(self.at(below), below, True).wait_recv()

            @pl.when(self.me < self.n - 1)
            def _():
                self.copy(self.at(below), below, True).start()

        @pl.when(above < self.n)
        def _():
            self.copy(self.at(above), above, False).wait_recv()

            @pl.when(self.me > 0)
            def _():
                self.copy(self.at(above), above, False).start()

    def finish(self):
        for origin in range(self.n):

            @pl.when(jnp.logical_and(origin <= self.me, self.me < self.n - 1))
            def _():
                self.copy(self.at(origin), origin, True).wait_send()

            @pl.when(jnp.logical_and(origin >= self.me, self.me > 0))
            def _():
                self.copy(self.at(origin), origin, False).wait_send()


class LineScatter:
    def __init__(self, ctx, me, n, partial, total, out, arrived, send, recv):
        self.ctx, self.me, self.n = ctx, me, n
        self.partial, self.total, self.out = partial, total, out
        self.arrived = arrived
        self.send, self.recv = send, recv

    def copy(self, t, up, slot):
        target = self.me + 1 if up else self.me - 1
        return pltpu.make_async_remote_copy(
            src_ref=self.out.at[t],
            dst_ref=self.arrived.at[slot],
            send_sem=self.send.at[t],
            recv_sem=self.recv.at[slot],
            device_id=(self.ctx, target),
            device_id_type=MESH,
        )

    def add(self, slot):
        self.copy(0, True, slot).wait_recv()
        self.total[...] += self.arrived[slot].astype(F32)

    def step(self, s):
        me, n = self.me, self.n

        @pl.when(s >= me)
        def _():
            t = n - 1 - s + me
            self.partial(t, self.total)

            @pl.when(me > 0)
            def _():
                self.add(t)

            self.out[t] = self.total[...].astype(BF16)

            @pl.when(s > me)
            def _():
                self.copy(t + 1, True, t + 1).wait_send()

            self.copy(t, True, t).start()

        @pl.when(s >= n - 1 - me)
        def _():
            t = s - (n - 1 - me)
            self.partial(t, self.total)

            @pl.when(me < n - 1)
            def _():
                self.add(t)

            self.out[t] = self.total[...].astype(BF16)

            @pl.when(s > n - 1 - me)
            def _():
                self.copy(t - 1, False, t - 1).wait_send()

            self.copy(t, False, n if s == n - 2 else t).start()

    def finish(self):
        me, n = self.me, self.n
        self.partial(me, self.total)

        @pl.when(me > 0)
        def _():
            self.add(me)

        @pl.when(me < n - 1)
        def _():
            self.add(n)

        @pl.when(me < n - 1)
        def _():
            self.copy(me + 1, True, me + 1).wait_send()

        @pl.when(me > 0)
        def _():
            self.copy(me - 1, False, me - 1).wait_send()


class StateSum:
    def __init__(self, ctx, me, chips, later, local, mine, pair, chip_sum, arrived, sems, turns):
        self.chip, self.core = ctx // 2, lax.rem(ctx, 2)
        self.sibling = ctx + 1 - 2 * self.core
        self.me, self.chips, self.later = me, chips, later
        self.local, self.mine, self.pair = local, mine, pair
        self.chip_sum, self.arrived = chip_sum, arrived
        self.sems, self.turns = sems, turns
        half = chip_sum.shape[0]
        self.half = pl.ds(pl.multiple_of(self.core * half, half), half)

    def pair_copy(self):
        return pltpu.make_async_remote_copy(
            src_ref=self.mine,
            dst_ref=self.pair,
            send_sem=self.sems.at[0, 0],
            recv_sem=self.sems.at[1, 0],
            device_id=(self.sibling, self.me),
            device_id_type=MESH,
        )

    def chip_copy(self, target, origin):
        return pltpu.make_async_remote_copy(
            src_ref=self.chip_sum,
            dst_ref=self.arrived.at[origin, self.half, :],
            send_sem=self.sems.at[0, target + 1],
            recv_sem=self.sems.at[1, origin + 1],
            device_id=(2 * target + self.core, self.me),
            device_id_type=MESH,
        )

    def core_copy(self, origin):
        piece = self.arrived.at[origin, self.half, :]
        return pltpu.make_async_remote_copy(
            src_ref=piece,
            dst_ref=piece,
            send_sem=self.turns.at[0, origin],
            recv_sem=self.turns.at[1, origin],
            device_id=(self.sibling, self.me),
            device_id_type=MESH,
        )

    def wanted(self, source, target):
        return source > target if self.later else source < target

    def start(self):
        self.mine[...] = self.local[...].astype(BF16)
        self.pair_copy().start()

    def spread(self):
        self.pair_copy().wait()
        own = self.local[self.half, :] + self.pair[self.half, :].astype(F32)
        self.chip_sum[...] = own.astype(BF16)
        for other in range(self.chips):

            @pl.when(self.wanted(self.chip, other))
            def _():
                self.chip_copy(other, self.chip).start()

    def hand_on(self):
        for other in range(self.chips):

            @pl.when(self.wanted(other, self.chip))
            def _():
                self.chip_copy(other, other).wait_recv()
                self.core_copy(other).start()

    def collect(self):
        near = self.core == (0 if self.later else 1)
        self.local[...] = jnp.where(near, self.pair[...].astype(F32), 0.0)
        for other in range(self.chips):

            @pl.when(self.wanted(other, self.chip))
            def _():
                self.core_copy(other).wait_recv()
                self.local[...] += self.arrived[other].astype(F32)

    def finish(self):
        for other in range(self.chips):

            @pl.when(self.wanted(other, self.chip))
            def _():
                self.core_copy(other).wait_send()

            @pl.when(self.wanted(self.chip, other))
            def _():
                self.chip_copy(other, self.chip).wait_send()


class SlabReduce:
    def __init__(self, ctx, me, chips, factor, left, parts, kept, stores, arrivals, sems):
        self.chip, self.core = ctx // 2, lax.rem(ctx, 2)
        self.sibling = ctx + 1 - 2 * self.core
        self.me, self.chips, self.factor = me, chips, factor
        self.left, self.parts, self.kept, self.stores = left, parts, kept, stores
        self.pair_in, self.near_in, self.far_in = arrivals
        self.pair_sems, self.near_sems, self.far_sems = sems
        self.m = self.near_in.shape[1] + 1
        self.slab, self.wide = self.far_in.shape[2:]
        low, high = lax.rem(self.chip, self.m), self.chip // self.m
        self.first, self.second = (low, high), (high, low)

    def chip_of(self, side, first, second):
        return second * self.m + first if side == 0 else first * self.m + second

    def held(self, side, start, size):
        ref, column = self.stores[side]
        depth = ref.shape[0]
        row = pl.multiple_of(lax.rem(start, depth), size)
        column = pl.multiple_of(start // depth * 2 * self.wide + column, self.wide)
        return ref.at[pl.ds(row, size), pl.ds(column, self.wide)]

    def near_out(self, side, j):
        size = self.m * self.slab
        return self.held(side, self.chips * self.slab + (j - 1) * size, size)

    def far_out(self, side, j):
        start = (self.chips + self.m * (self.m - 1) + j - 1) * self.slab
        return self.held(side, start, self.slab)

    def times(self, rows, side):
        right, base = self.parts[side]
        return dot(rows, right[:, base : base + self.wide]) * self.factor

    def one_slab(self, side, second):
        first = self.first[side]
        high, low = (second, first) if side == 0 else (first, second)
        value = self.times(self.left[high, low, self.core], side)
        at = pl.ds(pl.multiple_of(low * self.slab, self.slab), self.slab)
        value = value + self.pair_in[side, high, at, :].astype(F32)
        row = pl.multiple_of(second * self.slab, self.slab)
        for j in range(1, self.m):
            value = value + self.near_in[side, j - 1, pl.ds(row, self.slab), :].astype(F32)
        return value

    def pair_copy(self, side, k):
        size = self.m * self.slab
        return pltpu.make_async_remote_copy(
            src_ref=self.held(side, k * size, size),
            dst_ref=self.pair_in.at[side, k],
            send_sem=self.pair_sems.at[0, side, k],
            recv_sem=self.pair_sems.at[1, side, k],
            device_id=(self.sibling, self.me), device_id_type=MESH,
        )

    def near_copy(self, side, j):
        first = lax.rem(self.first[side] + j, self.m)
        target = self.chip_of(side, first, self.second[side])
        return pltpu.make_async_remote_copy(
            src_ref=self.near_out(side, j), dst_ref=self.near_in.at[side, j - 1],
            send_sem=self.near_sems.at[0, side, j], recv_sem=self.near_sems.at[1, side, j],
            device_id=(2 * target + self.core, self.me), device_id_type=MESH,
        )

    def far_copy(self, side, j):
        second = lax.rem(self.second[side] + j, self.m)
        target = self.chip_of(side, self.first[side], second)
        return pltpu.make_async_remote_copy(
            src_ref=self.far_out(side, j), dst_ref=self.far_in.at[side, j - 1],
            send_sem=self.far_sems.at[0, side, j], recv_sem=self.far_sems.at[1, side, j],
            device_id=(2 * target + self.core, self.me), device_id_type=MESH,
        )

    def to_pair(self):
        size = self.m * self.slab

        @pl.loop(0, self.m)
        def _(k):
            rows = self.left[k, :, 1 - self.core]
            rows = rows.reshape(size, rows.shape[-1])
            for side in range(2):
                self.held(side, k * size, size)[...] = self.times(rows, side).astype(BF16)
                self.pair_copy(side, k).start()

    def to_near(self):
        for side in range(2):
            @pl.loop(0, self.m)
            def _(k):
                self.pair_copy(side, k).wait_recv()

            @pl.loop(1, self.m)
            def _(j):
                first = lax.rem(self.first[side] + j, self.m)
                first_rows = pl.ds(pl.multiple_of(first * self.slab, self.slab), self.slab)
                if side == 0:
                    rows, pair = self.left[:, first, self.core], self.pair_in[side, :, first_rows]
                else:
                    rows, pair = self.left[first, :, self.core], self.pair_in[side, first]
                size = self.m * self.slab
                value = self.times(rows.reshape(size, rows.shape[-1]), side)
                value = value + pair.reshape(size, self.wide).astype(F32)
                self.near_out(side, j)[...] = value.astype(BF16)
                self.near_copy(side, j).start()

    def to_far(self):
        for side in range(2):

            @pl.loop(1, self.m)
            def _(j):
                self.near_copy(side, j).wait_recv()

            @pl.loop(1, self.m)
            def _(j):
                second = lax.rem(self.second[side] + j, self.m)
                self.far_out(side, j)[...] = self.one_slab(side, second).astype(BF16)
                self.far_copy(side, j).start()

    def keep_own(self):
        for side in range(2):
            ref, column = self.kept[side]
            ref[:, column : column + self.wide] = self.one_slab(side, self.second[side])

    def collect(self):
        for side in range(2):
            ref, column = self.kept[side]

            @pl.loop(1, self.m)
            def _(j):
                self.far_copy(side, j).wait_recv()
                ref[:, column : column + self.wide] += self.far_in[side, j - 1].astype(F32)

    def finish(self):
        for side in range(2):

            @pl.loop(0, self.m)
            def _(k):
                self.pair_copy(side, k).wait_send()

            @pl.loop(1, self.m)
            def _(j):
                self.near_copy(side, j).wait_send()
                self.far_copy(side, j).wait_send()


class Share:
    def __init__(self, ctx, me, partner, chips, source, held, send, recv):
        self.ctx, self.me, self.partner, self.chips = ctx, me, partner, chips
        self.chip, self.core = ctx // 2, lax.rem(ctx, 2)
        self.source, self.held, self.send, self.recv = source, held, send, recv

    def at(self, ref, origin):
        rows = self.held.shape[0] // (2 * self.chips)
        return ref.at[pl.ds(pl.multiple_of(origin * rows, rows), rows), :]

    def copy(self, source, origin, sem, target):
        return pltpu.make_async_remote_copy(
            src_ref=self.at(source, origin), dst_ref=self.at(self.held, origin),
            send_sem=self.send.at[sem], recv_sem=self.recv.at[origin],
            device_id=target, device_id_type=MESH,
        )

    def inward(self):
        return self.copy(self.source, self.ctx, 0, (self.ctx, self.partner))

    def to_chip(self, p):
        return self.copy(self.held, self.ctx, 1 + p, (2 * p + self.core, self.me))

    def to_sibling(self, p):
        target = (self.ctx + 1 - 2 * self.core, self.me)
        return self.copy(self.held, 2 * p + self.core, 1 + self.chips + p, target)

    def arrival(self, origin):
        self.copy(self.held, origin, 0, (self.ctx, self.partner)).wait_recv()

    def spread(self):
        self.arrival(self.ctx)

        @pl.loop(1, self.chips)
        def _(j):
            self.to_chip(lax.rem(self.chip + j, self.chips)).start()

        self.to_sibling(self.chip).start()

    def hand_on(self):
        @pl.loop(1, self.chips)
        def _(j):
            p = lax.rem(self.chip + self.chips - j, self.chips)
            self.arrival(2 * p + self.core)
            self.to_sibling(p).start()

    def complete(self):
        @pl.loop(0, self.chips)
        def _(p):
            self.arrival(2 * p + 1 - self.core)

    def finish(self):
        @pl.loop(0, self.chips)
        def _(p):
            self.to_sibling(p).wait_send()

        @pl.loop(1, self.chips)
        def _(j):
            self.to_chip(lax.rem(self.chip + j, self.chips)).wait_send()


def block_kernel(
    n, chips, factor,
    x_hbm, cot_hbm, in_gain_ref, gain_ref, w_hbm, wo_hbm,
    outputs_hbm, igrad_hbm, qgrad_hbm, ograd_hbm,
    outputs_ref, igrad_ref, qgrad_ref, ograd_ref,
    w_ref, wt_ref, both_wo, load,
    normt_ref, proj_ref, both_mixed, gproj_ref,
    x_ref, held_x, xsend, xrecv,
    held_c, cott_ref, csend, crecv,
    gm_ref, gsend, grecv, msend, mrecv, wsend, wrecv,
    total, po_ref, pi_ref, osend, orecv, og_ref, ogsem,
    back_out, back_in, bsend, brecv,
    scores, attended, gatt, gkey, gval,
    local_f, mine_f, pair_f, sum_f, arrived_f, sems_f, turns_f,
    local_b, mine_b, pair_b, sum_b, arrived_b, sems_b, turns_b,
    q0, q1, q2, q3, q4, q5, k0, k1, k2, k3, k4, k5,
    kept_p, o0, o1, o2, o3, o4, o5, p0, p1, p2, p3, p4, p5,
):
    ctx, me = lax.axis_index("ctx"), lax.axis_index("tp")
    rows = x_hbm.shape[0]
    block, width = both_mixed.shape[0], both_mixed.shape[1] // 2
    mixed_ref, mixp_ref = both_mixed.at[:, :width], both_mixed.at[:, width:]
    wo_ref, wop_ref = both_wo.at[:width], both_wo.at[width:]
    heads = width // DH
    chip, core = ctx // 2, lax.rem(ctx, 2)
    mate = me + 1 - 2 * lax.rem(me, 2)
    across = n - 1 - me
    beyond = n - 1 - mate
    edge = jnp.logical_or(me == 0, me == n - 1)
    inner = jnp.logical_not(edge)

    def store(source, target, sem):
        copy = pltpu.make_async_copy(source, target, load.at[sem])
        copy.start()
        return copy

    def row_at(origin):
        return pl.ds(pl.multiple_of(origin * rows, rows), rows)

    def cols(h, part=0):
        if isinstance(h, int):
            return slice(part * width + h * DH, part * width + (h + 1) * DH)
        return pl.ds(pl.multiple_of(part * width + h * DH, DH), DH)

    def head_rows(h):
        if isinstance(h, int):
            return slice(h * DH, (h + 1) * DH)
        return pl.ds(pl.multiple_of(h * DH, DH), DH)

    def each_head(body):
        for h in range(heads):
            body(h)

    def causal(value):
        down = lax.broadcasted_iota(jnp.int32, (block, block), 0)
        along = lax.broadcasted_iota(jnp.int32, (block, block), 1)
        return jnp.where(down >= along, value, 0.0).astype(BF16)

    x_load = pltpu.make_async_copy(x_hbm, x_ref, load.at[0])
    w_load = pltpu.make_async_copy(w_hbm, w_ref, load.at[1])
    c_load = pltpu.make_async_copy(cot_hbm, held_c.at[row_at(me), :], load.at[2])
    wo_load = pltpu.make_async_copy(wo_hbm, wo_ref, load.at[3])
    x_load.start()
    w_load.start()
    c_load.start()
    wo_load.start()
    others = [ctx + 1 - 2 * core]
    others += [2 * lax.rem(chip + j, chips) + core for j in range(1, chips)]
    line_barrier(ctx, me, n, others)
    gather_x = LineGather(ctx, me, n, x_hbm, held_x, xsend, xrecv)
    share = Share(ctx, me, mate, chips, wo_hbm, wop_ref, wsend, wrecv)
    forward = StateSum(
        ctx, me, chips, False, local_f, mine_f, pair_f, sum_f, arrived_f, sems_f, turns_f
    )
    backward = StateSum(
        ctx, me, chips, True, local_b, mine_b, pair_b, sum_b, arrived_b, sems_b, turns_b
    )
    half = width // 2
    reduce_q = SlabReduce(
        ctx, me, chips, factor, normt_ref, [(gproj_ref, 0), (gproj_ref, half)],
        [(qgrad_ref.at[0], 0), (qgrad_ref.at[0], half)],
        [(w_ref.at[1], 0), (w_ref.at[1], half)], (q0, q1, q2), (q3, q4, q5),
    )
    reduce_k = SlabReduce(
        ctx, me, chips, factor, normt_ref, [(gproj_ref, width), (gproj_ref, 2 * width)],
        [(qgrad_ref.at[1], 0), (qgrad_ref.at[2], 0)],
        [(w_ref.at[0], 0), (w_ref.at[2], 0)], (k0, k1, k2), (k3, k4, k5),
    )
    reduce_o = SlabReduce(
        ctx, me, chips, factor, cott_ref, [(mixed_ref, 0), (mixed_ref, half)],
        [(ograd_ref, 0), (ograd_ref, half)],
        [(w_ref.at[1], 0), (w_ref.at[1], half)], (o0, o1, o2), (o3, o4, o5),
    )
    reduce_p = SlabReduce(
        ctx, me, chips, factor, cott_ref, [(mixp_ref, 0), (mixp_ref, half)],
        [(kept_p, 0), (kept_p, half)],
        [(held_x, 0), (held_x, half)], (p0, p1, p2), (p3, p4, p5),
    )

    def remote(source, target, send, recv, device):
        return pltpu.make_async_remote_copy(
            src_ref=source, dst_ref=target, send_sem=send, recv_sem=recv,
            device_id=(ctx, device), device_id_type=MESH,
        )

    def cot_copy(source, origin, sem, device):
        return remote(
            source, held_c.at[row_at(origin), :], csend.at[sem], crecv.at[origin], device
        )

    def grad_copy(origin):
        piece = gm_ref.at[row_at(origin), :]
        return remote(piece, piece, gsend.at[origin], grecv.at[origin], mate)

    def mixed_copy(origin):
        at = row_at(origin)
        return remote(
            mixed_ref.at[at, :], mixp_ref.at[at, :], msend.at[origin], mrecv.at[origin], mate
        )

    def out_copy(slot, landing, device):
        return remote(
            po_ref.at[slot], pi_ref.at[landing], osend.at[slot], orecv.at[landing], device
        )

    def ograd_copy():
        return remote(og_ref, og_ref, ogsem.at[0], ogsem.at[1], mate)

    def project(source, origin):
        at = row_at(origin)
        piece = source[...].astype(F32)
        normed = (piece * row_scale(piece) * in_gain_ref[...]).astype(BF16)
        for part in range(3):
            here = slice(part * width, (part + 1) * width)
            proj_ref[at, here] = dot(normed, w_ref[part]).astype(BF16)
        normt_ref[:, :, :, :, at] = normed.T.reshape(normt_ref.shape[:4] + (rows,))

    def turn_weight(first, last):
        step = 2 * DH
        count = w_ref.shape[1] // step

        @pl.loop(first, last)
        def _(k):
            part = k // count
            at = pl.ds(pl.multiple_of(lax.rem(k, count) * step, step), step)
            into = pl.ds(pl.multiple_of(part * width, width), width)
            wt_ref[into, at] = w_ref[part, at, :].T

    gather_x.start_up()
    gather_x.start_down()
    x_load.wait()
    w_load.wait()
    project(x_ref, me)
    turns = 3 * w_ref.shape[1] // (2 * DH)
    turn_weight(0, turns // 2)

    @pl.loop(1, n)
    def _(d):
        @pl.when(jnp.logical_and(inner, d == 2))
        def _():
            share.spread()

        gather_x.step(d)

        @pl.when(jnp.logical_and(edge, d == 1))
        def _():
            share.inward().start()

        @pl.when(jnp.logical_and(inner, d == 2))
        def _():
            cot_copy(cot_hbm, me, 0, across).start()

        @pl.when(me - d >= 0)
        def _():
            project(gather_x.at(me - d), me - d)

        @pl.when(me + d < n)
        def _():
            project(gather_x.at(me + d), me + d)

        @pl.when(d == 1)
        def _():
            turn_weight(turns // 2, turns)

            @pl.when(edge)
            def _():
                share.inward().wait_send()
                cot_copy(cot_hbm, me, 0, mate).start()

    @each_head
    def _(h):
        local_f[head_rows(h), :] = dot(proj_ref[:, cols(h, 1)], proj_ref[:, cols(h, 2)], TN)

    forward.start()

    @each_head
    def _(h):
        scores[h] = causal(dot(proj_ref[:, cols(h)], proj_ref[:, cols(h, 1)], NT))

    forward.spread()

    @each_head
    def _(h):
        attended[:, cols(h)] = dot(scores[h], proj_ref[:, cols(h, 2)])

    wo_load.wait()
    c_load.wait()

    @pl.when(edge)
    def _():
        total[:, :width] = dot(held_c[row_at(me), :], wo_ref[...], NT)

    forward.hand_on()

    @pl.when(inner)
    def _():
        share.hand_on()
        cot_copy(cot_hbm, mate, 0, mate).wait_recv()
        cot_copy(held_c.at[row_at(mate), :], mate, 1, across).start()

    forward.collect()

    @each_head
    def _(h):
        query = proj_ref[:, cols(h)]
        value = attended[:, cols(h)] + with_state(query, local_f[head_rows(h), :])
        attended[:, cols(h)] = value
        mixed_ref[:, cols(h)] = (value * row_scale(value) * gain_ref[:, cols(h)]).astype(BF16)


    def grad_rows(at, value):
        weighted = value * gain_ref[...]
        for h in range(heads):
            here = slice(h * DH, (h + 1) * DH)
            value = attended[at, here]
            scale = row_scale(value)
            part = weighted[:, here]
            mean = jnp.mean(part * value, axis=-1, keepdims=True)
            gatt[at, here] = (scale * part - scale * scale * scale * value * mean).astype(BF16)

    def rows_from(origin, count=1):
        return pl.ds(pl.multiple_of(origin * rows, rows), count * rows)

    def own_rows(origin, count=1):
        at = rows_from(origin, count)
        grad_rows(at, dot(held_c[at, :], wo_ref[...], NT))

    def mate_rows(origin, count=1):
        at = rows_from(origin, count)
        gm_ref[at, :] = dot(held_c[at, :], wop_ref[...], NT).astype(BF16)
        for k in range(count):
            grad_copy(origin + k).start()

    def turn_cot(origin):
        at = row_at(origin)
        cott_ref[:, :, :, :, at] = held_c[at, :].T.reshape(cott_ref.shape[:4] + (rows,))

    low = me // 2
    last = (n - 1) * (1 - low)

    def attend_back(h, at, first, count):
        query, grad = proj_ref[at, cols(h)], gatt[at, cols(h)]
        key, value = proj_ref[:, cols(h, 1)], proj_ref[:, cols(h, 2)]
        down = lax.broadcasted_iota(jnp.int32, (count, block), 0) + first
        along = lax.broadcasted_iota(jnp.int32, (count, block), 1)
        raw = dot(grad, value, NT)
        gscores = jnp.where(down >= along, raw, 0.0).astype(BF16)
        gquery = dot(gscores, key) + with_state(grad, local_f[head_rows(h), :], NT)
        gproj_ref[at, cols(h)] = gquery.astype(BF16)
        return dot(gscores, query, TN), dot(scores[h, at, :], grad, TN)

    @pl.when(edge)
    def _():
        for origin in (across, beyond, mate, me):
            mixed_copy(origin).start()
        grad_rows(row_at(me), total[:, :width])
        for origin in (mate, beyond):
            grad_copy(origin).wait_recv()
        here = rows_from(1, n - 2)
        grad_rows(here, gm_ref[here, :].astype(F32))

    @pl.when(inner)
    def _():
        share.complete()
        cot_copy(cot_hbm, across, 0, across).wait_recv()
        mate_rows(1, n - 2)
        own_rows(me - 1, n - 1)

    most = rows_from(low, n - 1)

    @each_head
    def _(h):
        local_b[head_rows(h), :] = dot(proj_ref[most, cols(h)], gatt[most, cols(h)], TN)
        gk, gv = attend_back(h, most, low * rows, (n - 1) * rows)
        gkey[:, cols(h)] = gk
        gval[:, cols(h)] = gv

    @pl.when(edge)
    def _():
        grad_copy(across).wait_recv()
        grad_rows(row_at(across), gm_ref[row_at(across), :].astype(F32))

    @pl.when(inner)
    def _():
        turn_cot(me)
        turn_cot(mate)
        turn_cot(across)
        cot_copy(cot_hbm, beyond, 0, across).wait_recv()
        mate_rows(beyond)
        own_rows(beyond)

    @each_head
    def _(h):
        at = row_at(last)
        local_b[head_rows(h), :] += dot(proj_ref[at, cols(h)], gatt[at, cols(h)], TN)

    def out_mine(origin, into):
        into[...] = dot(mixed_ref[row_at(origin), :], wo_ref[...])

    def out_both(origin, into):
        into[...] = dot(both_mixed[row_at(origin), :], both_wo[...])

    backward.start()

    @pl.when(inner)
    def _():
        turn_cot(beyond)
        reduce_o.to_pair()

    backward.spread()

    @pl.when(inner)
    def _():
        reduce_o.to_near()
        for slot, origin in enumerate((beyond, across)):
            mixed_copy(origin).wait_recv()
            out_both(origin, total)
            po_ref[slot] = total[...].astype(BF16)
            out_copy(slot, slot, across).start()

    @each_head
    def _(h):
        gk, gv = attend_back(h, row_at(last), last * rows, rows)
        gkey[:, cols(h)] += gk
        gval[:, cols(h)] += gv

    backward.hand_on()
    gather_x.finish()

    @pl.when(inner)
    def _():
        mixed_copy(mate).wait_recv()
        mixed_copy(me).wait_recv()
        reduce_p.to_pair()
        reduce_o.to_far()
        reduce_p.to_near()

    backward.collect()

    @each_head
    def _(h):
        state = local_b[head_rows(h), :]
        key, value = proj_ref[:, cols(h, 1)], proj_ref[:, cols(h, 2)]
        gk = gkey[:, cols(h)] + with_state(value, state, NT)
        gv = gval[:, cols(h)] + with_state(key, state)
        gproj_ref[:, cols(h, 1)] = gk.astype(BF16)
        gproj_ref[:, cols(h, 2)] = gv.astype(BF16)

    def in_partial(t, into):
        into[...] = dot(gproj_ref[row_at(t), :], wt_ref[...])

    back = LineScatter(ctx, me, n, in_partial, total, back_out, back_in, bsend, brecv)
    back.step(0)

    @pl.when(inner)
    def _():
        reduce_o.finish()

    reduce_q.to_pair()
    reduce_q.to_near()
    reduce_k.to_pair()

    @pl.when(inner)
    def _():
        reduce_p.to_far()
        out_mine(mate, total)
        out_copy(0, 0, across).wait_recv()
        po_ref[2] = (total[...] + pi_ref[0].astype(F32)).astype(BF16)
        out_copy(2, 1, mate).start()

    reduce_k.to_near()
    back.step(1)

    @pl.when(inner)
    def _():
        reduce_p.keep_own()
        reduce_p.collect()
        og_ref[...] = kept_p[...].astype(BF16)
        ograd_copy().start()
        out_both(me, total)
        out_copy(1, 1, across).wait_recv()
        outputs_ref[...] = (
            x_ref[...].astype(F32) + total[...] + pi_ref[1].astype(F32)
        ).astype(BF16)
        reduce_o.keep_own()
        reduce_o.collect()

    reduce_q.to_far()
    reduce_q.keep_own()
    back.step(2)
    reduce_k.to_far()
    reduce_k.keep_own()

    @pl.when(edge)
    def _():
        out_mine(me, total)
        out_copy(2, 1, mate).wait_recv()
        outputs_ref[...] = (
            x_ref[...].astype(F32) + total[...] + pi_ref[1].astype(F32)
        ).astype(BF16)
        ograd_copy().wait_recv()
        ograd_ref[...] = og_ref[...].astype(F32)

    outputs_store = store(outputs_ref, outputs_hbm, 4)
    ograd_store = store(ograd_ref, ograd_hbm, 5)
    reduce_q.collect()
    reduce_k.collect()
    qgrad_store = store(qgrad_ref, qgrad_hbm, 6)
    back.finish()
    piece = x_ref[...].astype(F32)
    scale = row_scale(piece)
    weighted = total[...] * in_gain_ref[...]
    mean = jnp.mean(weighted * piece, axis=-1, keepdims=True)
    igrad_ref[...] = (
        held_c[row_at(me), :].astype(F32) + scale * weighted - scale * scale * scale * piece * mean
    ).astype(BF16)
    igrad_store = store(igrad_ref, igrad_hbm, 7)
    forward.finish()
    backward.finish()
    reduce_q.finish()
    reduce_k.finish()

    @pl.when(edge)
    def _():
        cot_copy(cot_hbm, me, 0, mate).wait_send()
        for origin in (across, beyond, mate, me):
            mixed_copy(origin).wait_send()

    @pl.when(inner)
    def _():
        share.finish()
        reduce_p.finish()
        cot_copy(cot_hbm, me, 0, across).wait_send()
        cot_copy(held_c.at[row_at(mate), :], mate, 1, across).wait_send()
        for origin in (me, across, beyond):
            grad_copy(origin).wait_send()
        out_copy(0, 0, across).wait_send()
        out_copy(1, 1, across).wait_send()
        out_copy(2, 1, mate).wait_send()
        ograd_copy().wait_send()
    for copy in (outputs_store, ograd_store, qgrad_store, igrad_store):
        copy.wait()


def hand_over(*refs):
    count = (len(refs) - 1) // 3
    sources, targets, held = refs[:count], refs[count : 2 * count], refs[2 * count : -1]
    sems = refs[-1]
    loads, stores = [], []
    for k in range(count):
        parts = sems.shape[2]
        for part in range(parts):
            axis = len(held[k].shape) - 2
            size = held[k].shape[axis] // parts
            at = (slice(None),) * axis + (pl.ds(part * size, size),)
            loads.append(pltpu.make_async_copy(sources[k].at[at], held[k].at[at], sems.at[0, k, part]))
            stores.append(pltpu.make_async_copy(held[k].at[at], targets[k].at[at], sems.at[1, k, part]))
    for copy in loads:
        copy.start()
    for k, copy in enumerate(loads):
        copy.wait()
        stores[k].start()
    for copy in stores:
        copy.wait()


def vmem(*shape, dtype=BF16):
    return pltpu.VMEM(shape, dtype)


def shards(inputs, norm_gain, qkv_weight, head_gain, out_weight, out_cotangent):
    rows, width = inputs.shape
    local_width = qkv_weight.shape[2]
    heads = local_width // DH
    n = lax.axis_size("tp")
    ctx_size = lax.axis_size("ctx")
    chips = ctx_size // 2
    block = rows * n
    slab = width // ctx_size
    factor = 1.0 / math.sqrt(block * ctx_size)
    dma = pltpu.SemaphoreType.DMA
    shape = jax.ShapeDtypeStruct
    m = math.isqrt(chips)
    state = [
        vmem(heads * DH, DH, dtype=F32),
        vmem(heads * DH, DH),
        vmem(heads * DH, DH),
        vmem(heads * DH // 2, DH),
        vmem(chips, heads * DH, DH),
        dma((2, chips + 1)),
        dma((2, chips)),
    ]

    def slabs(wide):
        return [
            vmem(2, m, m * slab, wide),
            vmem(2, m - 1, m * slab, wide),
            vmem(2, m - 1, slab, wide),
            dma((2, 2, m)),
            dma((2, 2, m)),
            dma((2, 2, m)),
        ]

    results = [
        shape((rows, width), BF16),
        shape((rows, width), BF16),
        shape((3, slab, local_width), F32),
        shape((slab, local_width), F32),
    ]
    staged = [vmem(*r.shape, dtype=r.dtype) for r in results]
    scratch = (
        staged
        + [vmem(3, width, local_width), vmem(3 * local_width, width)]
        + [vmem(2 * local_width, width), dma((8,))]
        + [vmem(m, m, 2, slab, block), vmem(block, 3 * local_width)]
        + [vmem(block, 2 * local_width), vmem(block, 3 * local_width)]
        + [vmem(rows, width), vmem(block, width), dma((2, n)), dma((n,))]
        + [vmem(block, width), vmem(m, m, 2, slab, block), dma((2,)), dma((n,))]
        + [vmem(block, local_width), dma((n,)), dma((n,)), dma((n,)), dma((n,))]
        + [dma((1 + 2 * chips,)), dma((ctx_size,))]
        + [vmem(rows, width, dtype=F32), vmem(3, rows, width), vmem(2, rows, width)]
        + [dma((3,)), dma((2,)), vmem(slab, local_width), dma((2,))]
        + [vmem(n, rows, width), vmem(n + 1, rows, width), dma((n,)), dma((n + 1,))]
        + [vmem(heads, block, block), vmem(block, local_width, dtype=F32)]
        + [vmem(block, local_width)]
        + [vmem(block, local_width, dtype=F32)] * 2
        + state
        + state
        + slabs(local_width // 2)
        + slabs(local_width)
        + [vmem(slab, local_width, dtype=F32)]
        + slabs(local_width // 2) * 2
    )
    held = pl.BlockSpec(memory_space=pltpu.VMEM)
    anywhere = pl.BlockSpec(memory_space=pl.ANY)
    made = pl.pallas_call(
        functools.partial(block_kernel, n, chips, factor),
        name="block",
        out_shape=results,
        in_specs=[anywhere] * 2 + [held] * 2 + [anywhere] * 2,
        out_specs=[anywhere] * 4,
        scratch_shapes=scratch,
        compiler_params=pltpu.CompilerParams(
            collective_id=0, has_side_effects=True, vmem_limit_bytes=VMEM_LIMIT
        ),
    )(
        inputs,
        out_cotangent,
        norm_gain.reshape(1, width),
        head_gain.reshape(1, local_width),
        qkv_weight.transpose(1, 0, 2),
        out_weight,
    )
    outputs, input_grad, qkv_grad, out_grad_t = pl.pallas_call(
        hand_over,
        name="hand_over",
        out_shape=results,
        in_specs=[anywhere] * 4,
        out_specs=[anywhere] * 4,
        scratch_shapes=staged + [dma((2, 4, 2))],
    )(*made)
    return (outputs, input_grad, qkv_grad.transpose(1, 0, 2), out_grad_t)


def solution(mesh):
    in_specs = (
        P(("ctx", "tp"), None),
        P(),
        P(None, None, "tp"),
        P("tp"),
        P("tp", None),
        P(("ctx", "tp"), None),
    )
    out_specs = (
        P(("ctx", "tp"), None),
        P(("ctx", "tp"), None),
        P("ctx", None, "tp"),
        P("ctx", "tp"),
    )
    return jax.shard_map(shards, mesh=mesh, in_specs=in_specs, out_specs=out_specs, check_vma=False)
```

```python
import functools
import math

import jax
import jax.numpy as jnp
from jax import lax
from jax.experimental import pallas as pl
from jax.experimental.pallas import tpu as pltpu
from jax.sharding import PartitionSpec as P

DH = 128
EPSILON = 1e-05
MESH = pl.DeviceIdType.MESH
F32 = jnp.float32
BF16 = jnp.bfloat16
VMEM_LIMIT = 63 * 1024 * 1024
NN = (((1,), (0,)), ((), ()))
NT = (((1,), (1,)), ((), ()))
TN = (((0,), (0,)), ((), ()))


def dot(a, b, dims=NN):
    return lax.dot_general(a, b, dims, preferred_element_type=F32)


def row_scale(rows):
    return lax.rsqrt(jnp.mean(rows * rows, axis=-1, keepdims=True) + EPSILON)


def split(value):
    high = value.astype(BF16)
    return high, (value - high.astype(F32)).astype(BF16)


def with_state(rows, state, dims=NN):
    return dot(
        jnp.concatenate([rows, rows], axis=1),
        jnp.concatenate(split(state), axis=dims[0][1][0]),
        dims,
    )


def line_barrier(ctx, me, n, others):
    barrier = pltpu.get_barrier_semaphore()

    @pl.when(me > 0)
    def _():
        pl.semaphore_signal(barrier, inc=1, device_id=(ctx, me - 1), device_id_type=MESH)

    @pl.when(me < n - 1)
    def _():
        pl.semaphore_signal(barrier, inc=1, device_id=(ctx, me + 1), device_id_type=MESH)

    for other in others:
        pl.semaphore_signal(barrier, inc=1, device_id=(other, me), device_id_type=MESH)
    inner = jnp.logical_and(me > 0, me < n - 1)

    @pl.when(inner)
    def _():
        pl.semaphore_wait(barrier, 2 + len(others))

    @pl.when(jnp.logical_not(inner))
    def _():
        pl.semaphore_wait(barrier, 1 + len(others))


class LineGather:
    def __init__(self, ctx, me, n, own, held, send, recv):
        self.ctx, self.me, self.n = ctx, me, n
        self.own, self.held, self.send, self.recv = own, held, send, recv

    def at(self, origin):
        rows = self.own.shape[0]
        return self.held.at[pl.ds(pl.multiple_of(origin * rows, rows), rows), :]

    def copy(self, source, origin, up):
        target = self.me + 1 if up else self.me - 1
        return pltpu.make_async_remote_copy(
            src_ref=source,
            dst_ref=self.at(origin),
            send_sem=self.send.at[1 if up else 0, origin],
            recv_sem=self.recv.at[origin],
            device_id=(self.ctx, target),
            device_id_type=MESH,
        )

    def start_up(self):
        @pl.when(self.me < self.n - 1)
        def _():
            self.copy(self.own, self.me, True).start()

    def start_down(self):
        @pl.when(self.me > 0)
        def _():
            self.copy(self.own, self.me, False).start()

    def step(self, d):
        below, above = self.me - d, self.me + d

        @pl.when(below >= 0)
        def _():
            self.copy(self.at(below), below, True).wait_recv()

            @pl.when(self.me < self.n - 1)
            def _():
                self.copy(self.at(below), below, True).start()

        @pl.when(above < self.n)
        def _():
            self.copy(self.at(above), above, False).wait_recv()

            @pl.when(self.me > 0)
            def _():
                self.copy(self.at(above), above, False).start()

    def finish(self):
        for origin in range(self.n):

            @pl.when(jnp.logical_and(origin <= self.me, self.me < self.n - 1))
            def _():
                self.copy(self.at(origin), origin, True).wait_send()

            @pl.when(jnp.logical_and(origin >= self.me, self.me > 0))
            def _():
                self.copy(self.at(origin), origin, False).wait_send()


class LineScatter:
    def __init__(self, ctx, me, n, partial, total, out, arrived, send, recv):
        self.ctx, self.me, self.n = ctx, me, n
        self.partial, self.total, self.out = partial, total, out
        self.arrived = arrived
        self.send, self.recv = send, recv

    def copy(self, t, up, slot):
        target = self.me + 1 if up else self.me - 1
        return pltpu.make_async_remote_copy(
            src_ref=self.out.at[t],
            dst_ref=self.arrived.at[slot],
            send_sem=self.send.at[t],
            recv_sem=self.recv.at[slot],
            device_id=(self.ctx, target),
            device_id_type=MESH,
        )

    def add(self, slot):
        self.copy(0, True, slot).wait_recv()
        self.total[...] += self.arrived[slot].astype(F32)

    def step(self, s):
        me, n = self.me, self.n

        @pl.when(s >= me)
        def _():
            t = n - 1 - s + me
            self.partial(t, self.total)

            @pl.when(me > 0)
            def _():
                self.add(t)

            self.out[t] = self.total[...].astype(BF16)

            @pl.when(s > me)
            def _():
                self.copy(t + 1, True, t + 1).wait_send()

            self.copy(t, True, t).start()

        @pl.when(s >= n - 1 - me)
        def _():
            t = s - (n - 1 - me)
            self.partial(t, self.total)

            @pl.when(me < n - 1)
            def _():
                self.add(t)

            self.out[t] = self.total[...].astype(BF16)

            @pl.when(s > n - 1 - me)
            def _():
                self.copy(t - 1, False, t - 1).wait_send()

            self.copy(t, False, n if s == n - 2 else t).start()

    def finish(self):
        me, n = self.me, self.n
        self.partial(me, self.total)

        @pl.when(me > 0)
        def _():
            self.add(me)

        @pl.when(me < n - 1)
        def _():
            self.add(n)

        @pl.when(me < n - 1)
        def _():
            self.copy(me + 1, True, me + 1).wait_send()

        @pl.when(me > 0)
        def _():
            self.copy(me - 1, False, me - 1).wait_send()


class StateSum:
    def __init__(self, ctx, me, chips, later, local, mine, pair, chip_sum, arrived, sems, turns):
        self.chip, self.core = ctx // 2, lax.rem(ctx, 2)
        self.sibling = ctx + 1 - 2 * self.core
        self.me, self.chips, self.later = me, chips, later
        self.local, self.mine, self.pair = local, mine, pair
        self.chip_sum, self.arrived = chip_sum, arrived
        self.sems, self.turns = sems, turns
        half = chip_sum.shape[0]
        self.half = pl.ds(pl.multiple_of(self.core * half, half), half)

    def pair_copy(self):
        return pltpu.make_async_remote_copy(
            src_ref=self.mine,
            dst_ref=self.pair,
            send_sem=self.sems.at[0, 0],
            recv_sem=self.sems.at[1, 0],
            device_id=(self.sibling, self.me),
            device_id_type=MESH,
        )

    def chip_copy(self, target, origin):
        return pltpu.make_async_remote_copy(
            src_ref=self.chip_sum,
            dst_ref=self.arrived.at[origin, self.half, :],
            send_sem=self.sems.at[0, target + 1],
            recv_sem=self.sems.at[1, origin + 1],
            device_id=(2 * target + self.core, self.me),
            device_id_type=MESH,
        )

    def core_copy(self, origin):
        piece = self.arrived.at[origin, self.half, :]
        return pltpu.make_async_remote_copy(
            src_ref=piece,
            dst_ref=piece,
            send_sem=self.turns.at[0, origin],
            recv_sem=self.turns.at[1, origin],
            device_id=(self.sibling, self.me),
            device_id_type=MESH,
        )

    def wanted(self, source, target):
        return source > target if self.later else source < target

    def start(self):
        self.mine[...] = self.local[...].astype(BF16)
        self.pair_copy().start()

    def spread(self):
        self.pair_copy().wait()
        own = self.local[self.half, :] + self.pair[self.half, :].astype(F32)
        self.chip_sum[...] = own.astype(BF16)
        for other in range(self.chips):

            @pl.when(self.wanted(self.chip, other))
            def _():
                self.chip_copy(other, self.chip).start()

    def hand_on(self):
        for other in range(self.chips):

            @pl.when(self.wanted(other, self.chip))
            def _():
                self.chip_copy(other, other).wait_recv()
                self.core_copy(other).start()

    def collect(self):
        near = self.core == (0 if self.later else 1)
        self.local[...] = jnp.where(near, self.pair[...].astype(F32), 0.0)
        for other in range(self.chips):

            @pl.when(self.wanted(other, self.chip))
            def _():
                self.core_copy(other).wait_recv()
                self.local[...] += self.arrived[other].astype(F32)

    def finish(self):
        for other in range(self.chips):

            @pl.when(self.wanted(other, self.chip))
            def _():
                self.core_copy(other).wait_send()

            @pl.when(self.wanted(self.chip, other))
            def _():
                self.chip_copy(other, self.chip).wait_send()


class SlabReduce:
    def __init__(self, ctx, me, chips, factor, left, parts, kept, stores, arrivals, sems):
        self.chip, self.core = ctx // 2, lax.rem(ctx, 2)
        self.sibling = ctx + 1 - 2 * self.core
        self.me, self.chips, self.factor = me, chips, factor
        self.left, self.parts, self.kept, self.stores = left, parts, kept, stores
        self.pair_in, self.near_in, self.far_in = arrivals
        self.pair_sems, self.near_sems, self.far_sems = sems
        self.m = self.near_in.shape[1] + 1
        self.slab, self.wide = self.far_in.shape[2:]
        low, high = lax.rem(self.chip, self.m), self.chip // self.m
        self.first, self.second = (low, high), (high, low)

    def chip_of(self, side, first, second):
        return second * self.m + first if side == 0 else first * self.m + second

    def held(self, side, start, size):
        ref, column = self.stores[side]
        depth = ref.shape[0]
        row = pl.multiple_of(lax.rem(start, depth), size)
        column = pl.multiple_of(start // depth * 2 * self.wide + column, self.wide)
        return ref.at[pl.ds(row, size), pl.ds(column, self.wide)]

    def near_out(self, side, j):
        size = self.m * self.slab
        return self.held(side, self.chips * self.slab + (j - 1) * size, size)

    def far_out(self, side, j):
        start = (self.chips + self.m * (self.m - 1) + j - 1) * self.slab
        return self.held(side, start, self.slab)

    def times(self, rows, side):
        right, base = self.parts[side]
        return dot(rows, right[:, base : base + self.wide]) * self.factor

    def one_slab(self, side, second):
        first = self.first[side]
        high, low = (second, first) if side == 0 else (first, second)
        value = self.times(self.left[high, low, self.core], side)
        at = pl.ds(pl.multiple_of(low * self.slab, self.slab), self.slab)
        value = value + self.pair_in[side, high, at, :].astype(F32)
        row = pl.multiple_of(second * self.slab, self.slab)
        for j in range(1, self.m):
            value = value + self.near_in[side, j - 1, pl.ds(row, self.slab), :].astype(F32)
        return value

    def pair_copy(self, side, k):
        size = self.m * self.slab
        return pltpu.make_async_remote_copy(
            src_ref=self.held(side, k * size, size),
            dst_ref=self.pair_in.at[side, k],
            send_sem=self.pair_sems.at[0, side, k],
            recv_sem=self.pair_sems.at[1, side, k],
            device_id=(self.sibling, self.me), device_id_type=MESH,
        )

    def near_copy(self, side, j):
        first = lax.rem(self.first[side] + j, self.m)
        target = self.chip_of(side, first, self.second[side])
        return pltpu.make_async_remote_copy(
            src_ref=self.near_out(side, j), dst_ref=self.near_in.at[side, j - 1],
            send_sem=self.near_sems.at[0, side, j], recv_sem=self.near_sems.at[1, side, j],
            device_id=(2 * target + self.core, self.me), device_id_type=MESH,
        )

    def far_copy(self, side, j):
        second = lax.rem(self.second[side] + j, self.m)
        target = self.chip_of(side, self.first[side], second)
        return pltpu.make_async_remote_copy(
            src_ref=self.far_out(side, j), dst_ref=self.far_in.at[side, j - 1],
            send_sem=self.far_sems.at[0, side, j], recv_sem=self.far_sems.at[1, side, j],
            device_id=(2 * target + self.core, self.me), device_id_type=MESH,
        )

    def to_pair(self):
        size = self.m * self.slab

        @pl.loop(0, self.m)
        def _(k):
            rows = self.left[k, :, 1 - self.core]
            rows = rows.reshape(size, rows.shape[-1])
            for side in range(2):
                self.held(side, k * size, size)[...] = self.times(rows, side).astype(BF16)
                self.pair_copy(side, k).start()

    def to_near(self):
        for side in range(2):
            @pl.loop(0, self.m)
            def _(k):
                self.pair_copy(side, k).wait_recv()

            @pl.loop(1, self.m)
            def _(j):
                first = lax.rem(self.first[side] + j, self.m)
                first_rows = pl.ds(pl.multiple_of(first * self.slab, self.slab), self.slab)
                if side == 0:
                    rows, pair = self.left[:, first, self.core], self.pair_in[side, :, first_rows]
                else:
                    rows, pair = self.left[first, :, self.core], self.pair_in[side, first]
                size = self.m * self.slab
                value = self.times(rows.reshape(size, rows.shape[-1]), side)
                value = value + pair.reshape(size, self.wide).astype(F32)
                self.near_out(side, j)[...] = value.astype(BF16)
                self.near_copy(side, j).start()

    def to_far(self):
        for side in range(2):

            @pl.loop(1, self.m)
            def _(j):
                self.near_copy(side, j).wait_recv()

            @pl.loop(1, self.m)
            def _(j):
                second = lax.rem(self.second[side] + j, self.m)
                self.far_out(side, j)[...] = self.one_slab(side, second).astype(BF16)
                self.far_copy(side, j).start()

    def keep_own(self):
        for side in range(2):
            ref, column = self.kept[side]
            ref[:, column : column + self.wide] = self.one_slab(side, self.second[side])

    def collect(self):
        for side in range(2):
            ref, column = self.kept[side]

            @pl.loop(1, self.m)
            def _(j):
                self.far_copy(side, j).wait_recv()
                ref[:, column : column + self.wide] += self.far_in[side, j - 1].astype(F32)

    def finish(self):
        for side in range(2):

            @pl.loop(0, self.m)
            def _(k):
                self.pair_copy(side, k).wait_send()

            @pl.loop(1, self.m)
            def _(j):
                self.near_copy(side, j).wait_send()
                self.far_copy(side, j).wait_send()


class Share:
    def __init__(self, ctx, me, partner, chips, source, held, send, recv):
        self.ctx, self.me, self.partner, self.chips = ctx, me, partner, chips
        self.chip, self.core = ctx // 2, lax.rem(ctx, 2)
        self.source, self.held, self.send, self.recv = source, held, send, recv

    def at(self, ref, origin):
        rows = self.held.shape[0] // (2 * self.chips)
        return ref.at[pl.ds(pl.multiple_of(origin * rows, rows), rows), :]

    def copy(self, source, origin, sem, target):
        return pltpu.make_async_remote_copy(
            src_ref=self.at(source, origin), dst_ref=self.at(self.held, origin),
            send_sem=self.send.at[sem], recv_sem=self.recv.at[origin],
            device_id=target, device_id_type=MESH,
        )

    def inward(self):
        return self.copy(self.source, self.ctx, 0, (self.ctx, self.partner))

    def to_chip(self, p):
        return self.copy(self.held, self.ctx, 1 + p, (2 * p + self.core, self.me))

    def to_sibling(self, p):
        target = (self.ctx + 1 - 2 * self.core, self.me)
        return self.copy(self.held, 2 * p + self.core, 1 + self.chips + p, target)

    def arrival(self, origin):
        self.copy(self.held, origin, 0, (self.ctx, self.partner)).wait_recv()

    def spread(self):
        self.arrival(self.ctx)

        @pl.loop(1, self.chips)
        def _(j):
            self.to_chip(lax.rem(self.chip + j, self.chips)).start()

        self.to_sibling(self.chip).start()

    def hand_on(self):
        @pl.loop(1, self.chips)
        def _(j):
            p = lax.rem(self.chip + self.chips - j, self.chips)
            self.arrival(2 * p + self.core)
            self.to_sibling(p).start()

    def complete(self):
        @pl.loop(0, self.chips)
        def _(p):
            self.arrival(2 * p + 1 - self.core)

    def finish(self):
        @pl.loop(0, self.chips)
        def _(p):
            self.to_sibling(p).wait_send()

        @pl.loop(1, self.chips)
        def _(j):
            self.to_chip(lax.rem(self.chip + j, self.chips)).wait_send()


def block_kernel(
    n, chips, factor,
    x_hbm, cot_hbm, in_gain_ref, gain_ref, w_hbm, wo_hbm,
    outputs_hbm, igrad_hbm, qgrad_hbm, ograd_hbm,
    outputs_ref, igrad_ref, qgrad_ref, ograd_ref,
    w_ref, wt_ref, both_wo, load,
    normt_ref, proj_ref, both_mixed, gproj_ref,
    x_ref, held_x, xsend, xrecv,
    held_c, cott_ref, csend, crecv,
    gm_ref, gsend, grecv, msend, mrecv, wsend, wrecv,
    total, po_ref, pi_ref, osend, orecv, og_ref, ogsem,
    back_out, back_in, bsend, brecv,
    scores, attended, gatt, gkey, gval,
    local_f, mine_f, pair_f, sum_f, arrived_f, sems_f, turns_f,
    local_b, mine_b, pair_b, sum_b, arrived_b, sems_b, turns_b,
    q0, q1, q2, q3, q4, q5, k0, k1, k2, k3, k4, k5,
    kept_p, o0, o1, o2, o3, o4, o5, p0, p1, p2, p3, p4, p5,
):
    ctx, me = lax.axis_index("ctx"), lax.axis_index("tp")
    rows = x_hbm.shape[0]
    block, width = both_mixed.shape[0], both_mixed.shape[1] // 2
    mixed_ref, mixp_ref = both_mixed.at[:, :width], both_mixed.at[:, width:]
    wo_ref, wop_ref = both_wo.at[:width], both_wo.at[width:]
    heads = width // DH
    chip, core = ctx // 2, lax.rem(ctx, 2)
    mate = me + 1 - 2 * lax.rem(me, 2)
    across = n - 1 - me
    beyond = n - 1 - mate
    edge = jnp.logical_or(me == 0, me == n - 1)
    inner = jnp.logical_not(edge)

    def store(source, target, sem):
        copy = pltpu.make_async_copy(source, target, load.at[sem])
        copy.start()
        return copy

    def row_at(origin):
        return pl.ds(pl.multiple_of(origin * rows, rows), rows)

    def cols(h, part=0):
        if isinstance(h, int):
            return slice(part * width + h * DH, part * width + (h + 1) * DH)
        return pl.ds(pl.multiple_of(part * width + h * DH, DH), DH)

    def head_rows(h):
        if isinstance(h, int):
            return slice(h * DH, (h + 1) * DH)
        return pl.ds(pl.multiple_of(h * DH, DH), DH)

    def each_head(body):
        for h in range(heads):
            body(h)

    def causal(value):
        down = lax.broadcasted_iota(jnp.int32, (block, block), 0)
        along = lax.broadcasted_iota(jnp.int32, (block, block), 1)
        return jnp.where(down >= along, value, 0.0).astype(BF16)

    x_load = pltpu.make_async_copy(x_hbm, x_ref, load.at[0])
    w_load = pltpu.make_async_copy(w_hbm, w_ref, load.at[1])
    c_load = pltpu.make_async_copy(cot_hbm, held_c.at[row_at(me), :], load.at[2])
    wo_load = pltpu.make_async_copy(wo_hbm, wo_ref, load.at[3])
    x_load.start()
    w_load.start()
    c_load.start()
    wo_load.start()
    others = [ctx + 1 - 2 * core]
    others += [2 * lax.rem(chip + j, chips) + core for j in range(1, chips)]
    line_barrier(ctx, me, n, others)
    gather_x = LineGather(ctx, me, n, x_hbm, held_x, xsend, xrecv)
    share = Share(ctx, me, mate, chips, wo_hbm, wop_ref, wsend, wrecv)
    forward = StateSum(
        ctx, me, chips, False, local_f, mine_f, pair_f, sum_f, arrived_f, sems_f, turns_f
    )
    backward = StateSum(
        ctx, me, chips, True, local_b, mine_b, pair_b, sum_b, arrived_b, sems_b, turns_b
    )
    half = width // 2
    reduce_q = SlabReduce(
        ctx, me, chips, factor, normt_ref, [(gproj_ref, 0), (gproj_ref, half)],
        [(qgrad_ref.at[0], 0), (qgrad_ref.at[0], half)],
        [(w_ref.at[1], 0), (w_ref.at[1], half)], (q0, q1, q2), (q3, q4, q5),
    )
    reduce_k = SlabReduce(
        ctx, me, chips, factor, normt_ref, [(gproj_ref, width), (gproj_ref, 2 * width)],
        [(qgrad_ref.at[1], 0), (qgrad_ref.at[2], 0)],
        [(w_ref.at[0], 0), (w_ref.at[2], 0)], (k0, k1, k2), (k3, k4, k5),
    )
    reduce_o = SlabReduce(
        ctx, me, chips, factor, cott_ref, [(mixed_ref, 0), (mixed_ref, half)],
        [(ograd_ref, 0), (ograd_ref, half)],
        [(w_ref.at[1], 0), (w_ref.at[1], half)], (o0, o1, o2), (o3, o4, o5),
    )
    reduce_p = SlabReduce(
        ctx, me, chips, factor, cott_ref, [(mixp_ref, 0), (mixp_ref, half)],
        [(kept_p, 0), (kept_p, half)],
        [(held_x, 0), (held_x, half)], (p0, p1, p2), (p3, p4, p5),
    )

    def remote(source, target, send, recv, device):
        return pltpu.make_async_remote_copy(
            src_ref=source, dst_ref=target, send_sem=send, recv_sem=recv,
            device_id=(ctx, device), device_id_type=MESH,
        )

    def cot_copy(source, origin, sem, device):
        return remote(
            source, held_c.at[row_at(origin), :], csend.at[sem], crecv.at[origin], device
        )

    def grad_copy(origin):
        piece = gm_ref.at[row_at(origin), :]
        return remote(piece, piece, gsend.at[origin], grecv.at[origin], mate)

    def mixed_copy(origin):
        at = row_at(origin)
        return remote(
            mixed_ref.at[at, :], mixp_ref.at[at, :], msend.at[origin], mrecv.at[origin], mate
        )

    def out_copy(slot, landing, device):
        return remote(
            po_ref.at[slot], pi_ref.at[landing], osend.at[slot], orecv.at[landing], device
        )

    def ograd_copy():
        return remote(og_ref, og_ref, ogsem.at[0], ogsem.at[1], mate)

    def project(source, origin):
        at = row_at(origin)
        piece = source[...].astype(F32)
        normed = (piece * row_scale(piece) * in_gain_ref[...]).astype(BF16)
        for part in range(3):
            here = slice(part * width, (part + 1) * width)
            proj_ref[at, here] = dot(normed, w_ref[part]).astype(BF16)
        normt_ref[:, :, :, :, at] = normed.T.reshape(normt_ref.shape[:4] + (rows,))

    def turn_weight(first, last):
        step = 2 * DH
        count = w_ref.shape[1] // step

        @pl.loop(first, last)
        def _(k):
            part = k // count
            at = pl.ds(pl.multiple_of(lax.rem(k, count) * step, step), step)
            into = pl.ds(pl.multiple_of(part * width, width), width)
            wt_ref[into, at] = w_ref[part, at, :].T

    gather_x.start_up()
    gather_x.start_down()
    x_load.wait()
    w_load.wait()
    project(x_ref, me)
    turns = 3 * w_ref.shape[1] // (2 * DH)
    turn_weight(0, turns // 2)

    @pl.loop(1, n)
    def _(d):
        @pl.when(jnp.logical_and(inner, d == 2))
        def _():
            share.spread()

        gather_x.step(d)

        @pl.when(jnp.logical_and(edge, d == 1))
        def _():
            share.inward().start()

        @pl.when(jnp.logical_and(inner, d == 2))
        def _():
            cot_copy(cot_hbm, me, 0, across).start()

        @pl.when(me - d >= 0)
        def _():
            project(gather_x.at(me - d), me - d)

        @pl.when(me + d < n)
        def _():
            project(gather_x.at(me + d), me + d)

        @pl.when(d == 1)
        def _():
            turn_weight(turns // 2, turns)

            @pl.when(edge)
            def _():
                share.inward().wait_send()
                cot_copy(cot_hbm, me, 0, mate).start()

    @each_head
    def _(h):
        local_f[head_rows(h), :] = dot(proj_ref[:, cols(h, 1)], proj_ref[:, cols(h, 2)], TN)

    forward.start()

    @each_head
    def _(h):
        scores[h] = causal(dot(proj_ref[:, cols(h)], proj_ref[:, cols(h, 1)], NT))

    forward.spread()

    @each_head
    def _(h):
        attended[:, cols(h)] = dot(scores[h], proj_ref[:, cols(h, 2)])

    wo_load.wait()
    c_load.wait()

    @pl.when(edge)
    def _():
        total[:, :width] = dot(held_c[row_at(me), :], wo_ref[...], NT)

    forward.hand_on()

    @pl.when(inner)
    def _():
        share.hand_on()
        cot_copy(cot_hbm, mate, 0, mate).wait_recv()
        cot_copy(held_c.at[row_at(mate), :], mate, 1, across).start()

    forward.collect()

    @each_head
    def _(h):
        query = proj_ref[:, cols(h)]
        value = attended[:, cols(h)] + with_state(query, local_f[head_rows(h), :])
        attended[:, cols(h)] = value
        mixed_ref[:, cols(h)] = (value * row_scale(value) * gain_ref[:, cols(h)]).astype(BF16)


    def grad_rows(at, value):
        weighted = value * gain_ref[...]
        for h in range(heads):
            here = slice(h * DH, (h + 1) * DH)
            value = attended[at, here]
            scale = row_scale(value)
            part = weighted[:, here]
            mean = jnp.mean(part * value, axis=-1, keepdims=True)
            gatt[at, here] = (scale * part - scale * scale * scale * value * mean).astype(BF16)

    def rows_from(origin, count=1):
        return pl.ds(pl.multiple_of(origin * rows, rows), count * rows)

    def own_rows(origin, count=1):
        at = rows_from(origin, count)
        grad_rows(at, dot(held_c[at, :], wo_ref[...], NT))

    def mate_rows(origin, count=1):
        at = rows_from(origin, count)
        gm_ref[at, :] = dot(held_c[at, :], wop_ref[...], NT).astype(BF16)
        for k in range(count):
            grad_copy(origin + k).start()

    def turn_cot(origin):
        at = row_at(origin)
        cott_ref[:, :, :, :, at] = held_c[at, :].T.reshape(cott_ref.shape[:4] + (rows,))

    low = me // 2
    last = (n - 1) * (1 - low)

    def attend_back(h, at, first, count):
        query, grad = proj_ref[at, cols(h)], gatt[at, cols(h)]
        key, value = proj_ref[:, cols(h, 1)], proj_ref[:, cols(h, 2)]
        down = lax.broadcasted_iota(jnp.int32, (count, block), 0) + first
        along = lax.broadcasted_iota(jnp.int32, (count, block), 1)
        raw = dot(grad, value, NT)
        gscores = jnp.where(down >= along, raw, 0.0).astype(BF16)
        gquery = dot(gscores, key) + with_state(grad, local_f[head_rows(h), :], NT)
        gproj_ref[at, cols(h)] = gquery.astype(BF16)
        return dot(gscores, query, TN), dot(scores[h, at, :], grad, TN)

    @pl.when(edge)
    def _():
        for origin in (across, beyond, mate, me):
            mixed_copy(origin).start()
        grad_rows(row_at(me), total[:, :width])
        for origin in (mate, beyond):
            grad_copy(origin).wait_recv()
        here = rows_from(1, n - 2)
        grad_rows(here, gm_ref[here, :].astype(F32))

    @pl.when(inner)
    def _():
        share.complete()
        cot_copy(cot_hbm, across, 0, across).wait_recv()
        mate_rows(1, n - 2)
        own_rows(me - 1, n - 1)

    most = rows_from(low, n - 1)

    @each_head
    def _(h):
        local_b[head_rows(h), :] = dot(proj_ref[most, cols(h)], gatt[most, cols(h)], TN)
        gk, gv = attend_back(h, most, low * rows, (n - 1) * rows)
        gkey[:, cols(h)] = gk
        gval[:, cols(h)] = gv

    @pl.when(edge)
    def _():
        grad_copy(across).wait_recv()
        grad_rows(row_at(across), gm_ref[row_at(across), :].astype(F32))

    @pl.when(inner)
    def _():
        turn_cot(me)
        turn_cot(mate)
        turn_cot(across)
        cot_copy(cot_hbm, beyond, 0, across).wait_recv()
        mate_rows(beyond)
        own_rows(beyond)

    @each_head
    def _(h):
        at = row_at(last)
        local_b[head_rows(h), :] += dot(proj_ref[at, cols(h)], gatt[at, cols(h)], TN)

    def out_mine(origin, into):
        into[...] = dot(mixed_ref[row_at(origin), :], wo_ref[...])

    def out_both(origin, into):
        into[...] = dot(both_mixed[row_at(origin), :], both_wo[...])

    backward.start()

    @pl.when(inner)
    def _():
        turn_cot(beyond)
        reduce_o.to_pair()

    backward.spread()

    @pl.when(inner)
    def _():
        reduce_o.to_near()
        for slot, origin in enumerate((beyond, across)):
            mixed_copy(origin).wait_recv()
            out_both(origin, total)
            po_ref[slot] = total[...].astype(BF16)
            out_copy(slot, slot, across).start()

    @each_head
    def _(h):
        gk, gv = attend_back(h, row_at(last), last * rows, rows)
        gkey[:, cols(h)] += gk
        gval[:, cols(h)] += gv

    backward.hand_on()
    gather_x.finish()

    @pl.when(inner)
    def _():
        mixed_copy(mate).wait_recv()
        mixed_copy(me).wait_recv()
        reduce_p.to_pair()
        reduce_o.to_far()
        reduce_p.to_near()

    backward.collect()

    @each_head
    def _(h):
        state = local_b[head_rows(h), :]
        key, value = proj_ref[:, cols(h, 1)], proj_ref[:, cols(h, 2)]
        gk = gkey[:, cols(h)] + with_state(value, state, NT)
        gv = gval[:, cols(h)] + with_state(key, state)
        gproj_ref[:, cols(h, 1)] = gk.astype(BF16)
        gproj_ref[:, cols(h, 2)] = gv.astype(BF16)

    def in_partial(t, into):
        into[...] = dot(gproj_ref[row_at(t), :], wt_ref[...])

    back = LineScatter(ctx, me, n, in_partial, total, back_out, back_in, bsend, brecv)
    back.step(0)

    @pl.when(inner)
    def _():
        reduce_o.finish()

    reduce_q.to_pair()
    reduce_q.to_near()
    reduce_k.to_pair()

    @pl.when(inner)
    def _():
        reduce_p.to_far()
        out_mine(mate, total)
        out_copy(0, 0, across).wait_recv()
        po_ref[2] = (total[...] + pi_ref[0].astype(F32)).astype(BF16)
        out_copy(2, 1, mate).start()

    reduce_k.to_near()
    back.step(1)

    @pl.when(inner)
    def _():
        reduce_p.keep_own()
        reduce_p.collect()
        og_ref[...] = kept_p[...].astype(BF16)
        ograd_copy().start()
        out_both(me, total)
        out_copy(1, 1, across).wait_recv()
        outputs_ref[...] = (
            x_ref[...].astype(F32) + total[...] + pi_ref[1].astype(F32)
        ).astype(BF16)

    reduce_q.to_far()
    back.step(2)
    reduce_k.to_far()

    @pl.when(inner)
    def _():
        reduce_o.keep_own()
        reduce_o.collect()

    reduce_q.keep_own()
    reduce_k.keep_own()

    @pl.when(edge)
    def _():
        out_mine(me, total)
        out_copy(2, 1, mate).wait_recv()
        outputs_ref[...] = (
            x_ref[...].astype(F32) + total[...] + pi_ref[1].astype(F32)
        ).astype(BF16)
        ograd_copy().wait_recv()
        ograd_ref[...] = og_ref[...].astype(F32)

    outputs_store = store(outputs_ref, outputs_hbm, 4)
    ograd_store = store(ograd_ref, ograd_hbm, 5)
    reduce_q.collect()
    reduce_k.collect()
    qgrad_store = store(qgrad_ref, qgrad_hbm, 6)
    back.finish()
    piece = x_ref[...].astype(F32)
    scale = row_scale(piece)
    weighted = total[...] * in_gain_ref[...]
    mean = jnp.mean(weighted * piece, axis=-1, keepdims=True)
    igrad_ref[...] = (
        held_c[row_at(me), :].astype(F32) + scale * weighted - scale * scale * scale * piece * mean
    ).astype(BF16)
    igrad_store = store(igrad_ref, igrad_hbm, 7)
    forward.finish()
    backward.finish()
    reduce_q.finish()
    reduce_k.finish()

    @pl.when(edge)
    def _():
        cot_copy(cot_hbm, me, 0, mate).wait_send()
        for origin in (across, beyond, mate, me):
            mixed_copy(origin).wait_send()

    @pl.when(inner)
    def _():
        share.finish()
        reduce_p.finish()
        cot_copy(cot_hbm, me, 0, across).wait_send()
        cot_copy(held_c.at[row_at(mate), :], mate, 1, across).wait_send()
        for origin in (me, across, beyond):
            grad_copy(origin).wait_send()
        out_copy(0, 0, across).wait_send()
        out_copy(1, 1, across).wait_send()
        out_copy(2, 1, mate).wait_send()
        ograd_copy().wait_send()
    for copy in (outputs_store, ograd_store, qgrad_store, igrad_store):
        copy.wait()


def hand_over(*refs):
    count = (len(refs) - 1) // 3
    sources, targets, held = refs[:count], refs[count : 2 * count], refs[2 * count : -1]
    sems = refs[-1]
    loads, stores = [], []
    for k in range(count):
        parts = sems.shape[2]
        for part in range(parts):
            axis = len(held[k].shape) - 2
            size = held[k].shape[axis] // parts
            at = (slice(None),) * axis + (pl.ds(part * size, size),)
            loads.append(pltpu.make_async_copy(sources[k].at[at], held[k].at[at], sems.at[0, k, part]))
            stores.append(pltpu.make_async_copy(held[k].at[at], targets[k].at[at], sems.at[1, k, part]))
    for copy in loads:
        copy.start()
    for k, copy in enumerate(loads):
        copy.wait()
        stores[k].start()
    for copy in stores:
        copy.wait()


def vmem(*shape, dtype=BF16):
    return pltpu.VMEM(shape, dtype)


def shards(inputs, norm_gain, qkv_weight, head_gain, out_weight, out_cotangent):
    rows, width = inputs.shape
    local_width = qkv_weight.shape[2]
    heads = local_width // DH
    n = lax.axis_size("tp")
    ctx_size = lax.axis_size("ctx")
    chips = ctx_size // 2
    block = rows * n
    slab = width // ctx_size
    factor = 1.0 / math.sqrt(block * ctx_size)
    dma = pltpu.SemaphoreType.DMA
    shape = jax.ShapeDtypeStruct
    m = math.isqrt(chips)
    state = [
        vmem(heads * DH, DH, dtype=F32),
        vmem(heads * DH, DH),
        vmem(heads * DH, DH),
        vmem(heads * DH // 2, DH),
        vmem(chips, heads * DH, DH),
        dma((2, chips + 1)),
        dma((2, chips)),
    ]

    def slabs(wide):
        return [
            vmem(2, m, m * slab, wide),
            vmem(2, m - 1, m * slab, wide),
            vmem(2, m - 1, slab, wide),
            dma((2, 2, m)),
            dma((2, 2, m)),
            dma((2, 2, m)),
        ]

    results = [
        shape((rows, width), BF16),
        shape((rows, width), BF16),
        shape((3, slab, local_width), F32),
        shape((slab, local_width), F32),
    ]
    staged = [vmem(*r.shape, dtype=r.dtype) for r in results]
    scratch = (
        staged
        + [vmem(3, width, local_width), vmem(3 * local_width, width)]
        + [vmem(2 * local_width, width), dma((8,))]
        + [vmem(m, m, 2, slab, block), vmem(block, 3 * local_width)]
        + [vmem(block, 2 * local_width), vmem(block, 3 * local_width)]
        + [vmem(rows, width), vmem(block, width), dma((2, n)), dma((n,))]
        + [vmem(block, width), vmem(m, m, 2, slab, block), dma((2,)), dma((n,))]
        + [vmem(block, local_width), dma((n,)), dma((n,)), dma((n,)), dma((n,))]
        + [dma((1 + 2 * chips,)), dma((ctx_size,))]
        + [vmem(rows, width, dtype=F32), vmem(3, rows, width), vmem(2, rows, width)]
        + [dma((3,)), dma((2,)), vmem(slab, local_width), dma((2,))]
        + [vmem(n, rows, width), vmem(n + 1, rows, width), dma((n,)), dma((n + 1,))]
        + [vmem(heads, block, block), vmem(block, local_width, dtype=F32)]
        + [vmem(block, local_width)]
        + [vmem(block, local_width, dtype=F32)] * 2
        + state
        + state
        + slabs(local_width // 2)
        + slabs(local_width)
        + [vmem(slab, local_width, dtype=F32)]
        + slabs(local_width // 2) * 2
    )
    held = pl.BlockSpec(memory_space=pltpu.VMEM)
    anywhere = pl.BlockSpec(memory_space=pl.ANY)
    made = pl.pallas_call(
        functools.partial(block_kernel, n, chips, factor),
        name="block",
        out_shape=results,
        in_specs=[anywhere] * 2 + [held] * 2 + [anywhere] * 2,
        out_specs=[anywhere] * 4,
        scratch_shapes=scratch,
        compiler_params=pltpu.CompilerParams(
            collective_id=0, has_side_effects=True, vmem_limit_bytes=VMEM_LIMIT
        ),
    )(
        inputs,
        out_cotangent,
        norm_gain.reshape(1, width),
        head_gain.reshape(1, local_width),
        qkv_weight.transpose(1, 0, 2),
        out_weight,
    )
    outputs, input_grad, qkv_grad, out_grad_t = pl.pallas_call(
        hand_over,
        name="hand_over",
        out_shape=results,
        in_specs=[anywhere] * 4,
        out_specs=[anywhere] * 4,
        scratch_shapes=staged + [dma((2, 4, 2))],
    )(*made)
    return (outputs, input_grad, qkv_grad.transpose(1, 0, 2), out_grad_t)


def solution(mesh):
    in_specs = (
        P(("ctx", "tp"), None),
        P(),
        P(None, None, "tp"),
        P("tp"),
        P("tp", None),
        P(("ctx", "tp"), None),
    )
    out_specs = (
        P(("ctx", "tp"), None),
        P(("ctx", "tp"), None),
        P("ctx", None, "tp"),
        P("ctx", "tp"),
    )
    return jax.shard_map(shards, mesh=mesh, in_specs=in_specs, out_specs=out_specs, check_vma=False)
```
